32 devices in a mesh: pairs: 2 (over y), rows: 8 (over z, x), cols: 2 (over core).
Axes of the slice: x: 2, y: 2, z: 4, core: 2. Of those that a mesh axis runs over, the one named last changes fastest.
Arguments:
- left_image: bfloat16 [32, 1024, 128], P(('pairs', 'rows'), 'cols'), parts along dimension 0, may hold values from -6 to 6
- right_image: bfloat16 [32, 1024, 128], P(('pairs', 'rows'), 'cols'), parts along dimension 0, may hold values from -6 to 6
- weight: bfloat16 [1152, 256], replicated, may hold values from -0.1875 to 0.1875
- level_zero: bfloat16 [32, 1024, 256], P(('pairs', 'rows'), 'cols'), parts along dimension 0, may hold values from -6 to 6
- level_one: bfloat16 [32, 1024, 128], P(('pairs', 'rows'), 'cols'), parts along dimension 0, may hold values from -6 to 6
- level_two: bfloat16 [32, 1024, 64], P(('pairs', 'rows'), 'cols'), parts along dimension 0, may hold values from -6 to 6
- level_three: bfloat16 [32, 1024, 32], P(('pairs', 'rows'), 'cols'), parts along dimension 0, may hold values from -6 to 6
Outputs:
- grad_left_in: bfloat16 [32, 1024, 128], P(('pairs', 'rows'), 'cols'), parts along dimension 0
- grad_right_in: bfloat16 [32, 1024, 128], P(('pairs', 'rows'), 'cols'), parts along dimension 0
- weight_grad: float32 [512, 1152], P(('pairs', 'rows')), parts along dimension 0
The draws below stay inside these ranges and needn't reach their ends.
There are 2 independent parts, one for each index of `pairs`. The reference program is written for one: setup_inputs(seed, part) draws one part's arguments, and reference() takes and returns one part's arrays. A program takes and returns all parts, laid end to end along the dimension named above; an argument that names none is the same for every part. Nothing has to cross between parts.
All inputs are finite; a program needn't handle non-finite values.
Results may differ from the reference program's by a relative error of at most 0.008.
Values may be sent and summed in bfloat16 or wider, within the bound.
A program may use at most 64 MiB of HBM per device.

```python
import math
import jax
import jax.numpy as jnp

DISP = 256
C = 256
CIN = 128
H = 16
W = 1024


def block_levels(key, dims, shards, low, high):
    def one(axis_at, parts):
        steps = jax.random.uniform(jax.random.fold_in(jax.random.fold_in(key, 6), axis_at), (parts,), jnp.float32, low / len(shards), high / len(shards))
        return jnp.repeat(jnp.exp(steps), dims[axis_at] // parts).reshape((-1,) + (1,) * (len(dims) - axis_at - 1))

    factor_of = one(*shards[0])
    for cut in shards[1:]:
        factor_of = factor_of * one(*cut)
    return factor_of


def scatter_about(stream_key, dims, deviation, reach, cuts=(), dtype=jnp.bfloat16):
    array = deviation * jax.random.normal(stream_key, dims, jnp.float32)
    if cuts:
        array = array * block_levels(stream_key, dims, cuts, -0.22, 0.18)
    return jnp.clip(array, -reach, reach).astype(dtype)


def setup_inputs(seed: int = 0, part: int = 0) -> dict:
    seeds = jax.random.split(jax.random.key(seed), 8)
    own_keys = jax.random.split(jax.random.fold_in(seeds[7], part), 8)
    left_image = scatter_about(own_keys[0], (H, W, CIN), 1.0, 6.0, ((0, 8), (1, 2)))
    right_image = scatter_about(own_keys[1], (H, W, CIN), 1.0, 6.0, ((0, 8), (1, 2)))
    weight = scatter_about(seeds[2], (9 * CIN, C), (9 * CIN) ** -0.5, 0.1875)
    level_zero = scatter_about(own_keys[3], (H, W, DISP), 1.0, 6.0, ((0, 8), (1, 2)))
    level_one = scatter_about(own_keys[4], (H, W, DISP // 2), 1.0, 6.0, ((0, 8), (1, 2)))
    level_two = scatter_about(own_keys[5], (H, W, DISP // 4), 1.0, 6.0, ((0, 8), (1, 2)))
    level_three = scatter_about(own_keys[6], (H, W, DISP // 8), 1.0, 6.0, ((0, 8), (1, 2)))
    return dict(left_image=left_image, right_image=right_image, weight=weight, level_zero=level_zero, level_one=level_one, level_two=level_two, level_three=level_three)


def skewed(band_rev):
    depth, count, width = band_rev.shape
    padded = jnp.pad(band_rev, ((0, 0), (0, 0), (0, count)))
    flat = padded.reshape(depth, count * (width + count))[:, :count * (width + count - 1)]
    return flat.reshape(depth, count, width + count - 1)

def combined_grad(level_zero, level_one, level_two, level_three):
    total = level_zero.astype(jnp.float32)
    total = total + jnp.repeat(level_one.astype(jnp.float32), 2, axis=-1) * 0.5
    total = total + jnp.repeat(level_two.astype(jnp.float32), 4, axis=-1) * 0.25
    total = total + jnp.repeat(level_three.astype(jnp.float32), 8, axis=-1) * 0.125
    return total.astype(jnp.bfloat16)

def reference(left_image, right_image, weight, level_zero, level_one, level_two, level_three):
    images = jnp.stack([left_image, right_image])
    framed = jnp.pad(images, ((0, 0), (1, 1), (1, 1), (0, 0)))
    out_sum = jnp.zeros((2 * H * W, C), jnp.float32)
    for row_tap in range(3):
        for col_tap in range(3):
            index = row_tap * 3 + col_tap
            taken = framed[:, row_tap:row_tap + H, col_tap:col_tap + W].reshape(-1, CIN)
            out_sum = out_sum + jnp.dot(taken, weight[index * CIN:(index + 1) * CIN], preferred_element_type=jnp.float32)
    feats = out_sum.astype(jnp.bfloat16).reshape(2, H, W, C)
    left_feat = feats[0]
    right_feat = feats[1]
    corr_grad = combined_grad(level_zero, level_one, level_two, level_three)
    edge = DISP - 1
    right_ext = jnp.pad(right_feat, ((0, 0), (edge, 0), (0, 0)))
    ext_grad = jnp.zeros((H, W + edge, C), jnp.float32)
    lefts = []
    for start in range(0, W, DISP):
        matrix = skewed(corr_grad[:, start:start + DISP, ::-1]).astype(jnp.float32)
        window = right_ext[:, start:start + DISP + edge].astype(jnp.float32)
        lefts.append(jnp.einsum('rik,rkc->ric', matrix, window))
        block_left = left_feat[:, start:start + DISP].astype(jnp.float32)
        ext_grad = ext_grad.at[:, start:start + DISP + edge].add(jnp.einsum('rik,ric->rkc', matrix, block_left))
    inverse = 1.0 / math.sqrt(C)
    left_grad = (jnp.concatenate(lefts, axis=1) * inverse).astype(jnp.bfloat16)
    right_grad = (ext_grad[:, edge:] * inverse).astype(jnp.bfloat16)
    feat_grad = jnp.stack([left_grad, right_grad])
    bordered = jnp.pad(feat_grad, ((0, 0), (1, 1), (1, 1), (0, 0)))
    flat_grad = feat_grad.reshape(-1, C)
    back_sum = jnp.zeros((2 * H * W, CIN), jnp.float32)
    pieces = []
    for row_tap in range(3):
        for col_tap in range(3):
            index = row_tap * 3 + col_tap
            taps_w = weight[index * CIN:(index + 1) * CIN]
            shifted = bordered[:, 2 - row_tap:2 - row_tap + H, 2 - col_tap:2 - col_tap + W].reshape(-1, C)
            back_sum = back_sum + jnp.dot(shifted, taps_w.T, preferred_element_type=jnp.float32)
            taken = framed[:, row_tap:row_tap + H, col_tap:col_tap + W].reshape(-1, CIN)
            pieces.append(jnp.dot(flat_grad.T, taken, preferred_element_type=jnp.float32))
    grad_pair = back_sum.astype(jnp.bfloat16).reshape(2, H, W, CIN)
    scale = 1.0 / math.sqrt(2 * H * W)
    weight_grad = jnp.concatenate(pieces, axis=1) * scale
    return (grad_pair[0], grad_pair[1], weight_grad)
```

```python
import functools
import math

import jax
import jax.numpy as jnp
from jax import lax
from jax.experimental import pallas as pl
from jax.experimental.pallas import tpu as pltpu
from jax.sharding import PartitionSpec as P

F32 = jnp.float32
BF16 = jnp.bfloat16
TILE = 16


def remote(src, dst, send, recv, row, col):
    return pltpu.make_async_remote_copy(
        src_ref=src,
        dst_ref=dst,
        send_sem=send,
        recv_sem=recv,
        device_id={"rows": row, "cols": col},
        device_id_type=pl.DeviceIdType.MESH,
    )


def matmul(a, b, dims):
    return lax.dot_general(a, b, (dims, ((), ())), preferred_element_type=F32)


def expansion(levels, reach, factor):
    source = lax.broadcasted_iota(jnp.int32, (levels, reach), 0)
    target = (reach - 1) - lax.broadcasted_iota(jnp.int32, (levels, reach), 1)
    bits = factor.bit_length() - 1
    hit = lax.shift_right_logical(target, jnp.int32(bits)) == source
    return jnp.where(hit, 1.0 / factor, 0.0).astype(BF16)


def kernel(
    rows, cols, left_hbm, right_hbm, weight_hbm, l0_hbm, l1_hbm, l2_hbm, l3_hbm, gl_out, gr_out, wg_out,
    left, right, gl_buf, gr_buf, wg_buf, weight, l0, l1, l2, l3, halo_row, halo_col, band_m, patch, left_feat, right_ext, ret_out, ret_in,
    grad, grad_edge, zed, part_out, part_in, acc, early, pair_out, pair_in, chunk, landed, whole,
    row_send, row_recv, col_send, col_recv, ext_send, ext_recv, ret_send, ret_recv,
    edge_send, edge_recv, part_send, part_recv, pair_send, pair_recv, chunk_send, chunk_recv, whole_send, whole_recv, load_sem, store_sem, known,
):
    depth, band, cin = left.shape
    features = weight.shape[1]
    reach = l0.shape[2]
    blocks = band // reach
    quota = features // (rows * cols)
    r = lax.axis_index("rows")
    c = lax.axis_index("cols")
    other = 1 - c
    images = (left, right)
    sources = (left_hbm, right_hbm)
    group = rows * cols
    has_up = r > 0
    has_down = r < rows - 1

    barrier = pltpu.get_barrier_semaphore()

    def tell(semaphore, row, col):
        pl.semaphore_signal(
            semaphore, inc=1, device_id={"rows": row, "cols": col}, device_id_type=pl.DeviceIdType.MESH
        )

    tell(barrier, r, other)

    @pl.when(has_up)
    def _():
        for col in (c, other):
            tell(barrier, r - 1, col)

    @pl.when(has_down)
    def _():
        for col in (c, other):
            tell(barrier, r + 1, col)

    loads = [
        pltpu.make_async_copy(src, dst, load_sem.at[k])
        for k, (src, dst) in enumerate(
            (
                (l0_hbm, l0), (l1_hbm, l1), (l2_hbm, l2), (l3_hbm, l3),
                (right_hbm, right), (left_hbm, left), (weight_hbm, weight),
            )
        )
    ]
    for load in loads:
        load.start()
    pl.semaphore_wait(barrier, 1 + 2 * has_up.astype(jnp.int32) + 2 * has_down.astype(jnp.int32))

    rounds = (rows - 1).bit_length()

    def spread_word(k):
        @pl.when(r >= 2**k)
        def _():
            tell(known.at[k, 1], r - 2**k, c)

        @pl.when(r + 2**k < rows)
        def _():
            tell(known.at[k, 0], r + 2**k, c)

    def hear_word(k):
        @pl.when(r >= 2**k)
        def _():
            pl.semaphore_wait(known.at[k, 0], 1)

        @pl.when(r + 2**k < rows)
        def _():
            pl.semaphore_wait(known.at[k, 1], 1)

    near = pl.multiple_of(other * (band - TILE), TILE)

    def down(i):
        return remote(sources[i].at[depth - 1], halo_row.at[0, i], row_send.at[0, i], row_recv.at[0, i], r + 1, c)

    def up(i):
        return remote(sources[i].at[0], halo_row.at[1, i], row_send.at[1, i], row_recv.at[1, i], r - 1, c)

    def tile_mid(i):
        return remote(
            sources[i].at[:, pl.ds(near, TILE)], halo_col.at[i, pl.ds(1, depth)],
            col_send.at[0, i], col_recv.at[0, i], r, other,
        )

    def tile_down(i):
        return remote(
            sources[i].at[depth - 1, pl.ds(near, TILE)], halo_col.at[i, 0],
            col_send.at[1, i], col_recv.at[1, i], r + 1, other,
        )

    def tile_up(i):
        return remote(
            sources[i].at[0, pl.ds(near, TILE)], halo_col.at[i, depth + 1],
            col_send.at[2, i], col_recv.at[2, i], r - 1, other,
        )

    for i in (1, 0):
        tile_mid(i).start()

    @pl.when(has_down)
    def _():
        for i in (1, 0):
            tile_down(i).start()
            down(i).start()

    spread_word(0)

    @pl.when(r == 0)
    def _():
        halo_row[0] = jnp.zeros_like(halo_row[0])
        for i in (0, 1):
            halo_col[i, 0] = jnp.zeros_like(halo_col[i, 0])

    @pl.when(r == rows - 1)
    def _():
        halo_row[1] = jnp.zeros_like(halo_row[1])
        for i in (0, 1):
            halo_col[i, depth + 1] = jnp.zeros_like(halo_col[i, depth + 1])

    spread = [expansion(count, reach, reach // count) for count in (reach, l1.shape[2], l2.shape[1], l3.shape[1])]
    for load in loads[:4]:
        load.wait()
    for h in range(depth):
        for s in range(blocks):
            at = pl.ds(s * reach, reach)
            total = matmul(l0[h, at], spread[0], ((1,), (0,)))
            total = total + matmul(l1[h, at], spread[1], ((1,), (0,)))
            for level, way in zip((l2, l3), spread[2:]):
                total = total + matmul(level[h, :, at], way, ((0,), (0,)))
            total = total.astype(BF16).astype(F32)
            wide = jnp.concatenate([total, jnp.zeros_like(total)], axis=1)
            band_m[h, s] = pltpu.roll(wide, 1, 1, stride=1, stride_axis=0).astype(BF16)

    place = lax.broadcasted_iota(jnp.int32, (band, cin), 0)

    def shifted(x, by, edge):
        if by == 1:
            return jnp.where(place == 0, edge, pltpu.roll(x, 1, 0))
        return jnp.where(place == band - 1, edge, pltpu.roll(x, band - 1, 0))

    def lay(framed, i):
        if framed == 0:
            base = halo_row[0, i]
        elif framed == depth + 1:
            base = halo_row[1, i]
        else:
            base = images[i][framed - 1]
        tile = halo_col[i, framed].astype(F32)
        zero = jnp.zeros((1, cin), F32)
        enter_left = jnp.where(c == 0, zero, tile[TILE - 1 : TILE])
        enter_right = jnp.where(c == 0, tile[0:1], zero)
        wide = base.astype(F32)
        three = (
            shifted(wide, 1, enter_left).astype(BF16),
            base,
            shifted(wide, -1, enter_right).astype(BF16),
        )
        for row_tap in range(3):
            h = framed - row_tap
            if 0 <= h < depth:
                for k in range(3):
                    patch[i, h, :, pl.ds((row_tap * 3 + k) * cin, cin)] = three[k]

    for load in loads[4:]:
        load.wait()
    for i in (1, 0):
        tile_mid(i).wait_recv()
        for framed in range(1, depth + 1):
            lay(framed, i)

    @pl.when(has_down)
    def _():
        for i in (1, 0):
            tile_down(i).wait_send()
            down(i).wait_send()

    @pl.when(has_up)
    def _():
        for i in (1, 0):
            tile_up(i).start()
            up(i).start()

    hear_word(0)
    if rounds > 1:
        spread_word(1)

    inverse = 1.0 / math.sqrt(features)

    def ext_copy(h):
        return remote(
            right_ext.at[h, pl.ds(band, reach)], right_ext.at[h, pl.ds(0, reach)],
            ext_send.at[h], ext_recv.at[h], r, other,
        )

    def ret_copy(h):
        return remote(ret_out.at[h], ret_in.at[h], ret_send.at[h], ret_recv.at[h], r, other)

    def edge_copy(h):
        return remote(
            grad.at[:, h, pl.ds(near, TILE)], grad_edge.at[:, h], edge_send.at[h], edge_recv.at[h], r, other
        )

    def part_copy(side, i):
        target = r - 1 if side == 0 else r + 1
        return remote(
            part_out.at[side, i], part_in.at[1 - side, i], part_send.at[side, i], part_recv.at[1 - side, i],
            target, c,
        )

    @pl.when(c == 0)
    def _():
        right_ext[:, 0:reach] = jnp.zeros((depth, reach, features), BF16)

    def process(h, ready):
        ready(1)
        feat = matmul(patch[1, h], weight[...], ((1,), (0,)))
        right_ext[h, pl.ds(reach, band)] = feat.astype(BF16)

        @pl.when(c == 0)
        def _():
            ext_copy(h).start()

        ready(0)
        left_feat[...] = matmul(patch[0, h], weight[...], ((1,), (0,))).astype(BF16)
        pending = None
        for s in range(blocks):
            both = matmul(band_m[h, s], left_feat[pl.ds(s * reach, reach)], ((0,), (0,)))
            head = both[:reach]
            if s == 0:
                ret_out[h] = head.astype(BF16)

                @pl.when(c == 1)
                def _():
                    ret_copy(h).start()
            else:
                grad[1, h, pl.ds((s - 1) * reach, reach)] = ((pending + head) * inverse).astype(BF16)
            pending = both[reach:]

        for s in range(blocks - 1, -1, -1):
            if s == 0:

                @pl.when(c == 1)
                def _():
                    ext_copy(h).wait_recv()

            window = right_ext[h, pl.ds(s * reach, 2 * reach)]
            out = matmul(band_m[h, s], window, ((1,), (0,)))
            grad[0, h, pl.ds(s * reach, reach)] = (out * inverse).astype(BF16)

        @pl.when(c == 0)
        def _():
            ret_copy(h).wait_recv()

        came = jnp.where(c == 0, ret_in[h].astype(F32), 0.0)
        grad[1, h, pl.ds(band - reach, reach)] = ((pending + came) * inverse).astype(BF16)
        edge_copy(h).start()
        for i in (0, 1):
            zed[i, h, 0:band] = matmul(grad[i, h], weight[...], ((1,), (1,)))
        edge_copy(h).wait_recv()
        for i in (0, 1):
            zed[i, h, pl.ds(band, TILE)] = matmul(grad_edge[i, h], weight[...], ((1,), (1,)))

    def weight_term(h, k):
        lanes = pl.ds(k * 3 * cin, 3 * cin)
        return matmul(grad[0, h], patch[0, h, :, lanes], ((0,), (0,))) + matmul(
            grad[1, h], patch[1, h, :, lanes], ((0,), (0,))
        )

    def gathered(i, goal):
        total = None
        for b in (0, 1, -1):
            inner = None
            enter = None
            for a in (-1, 0, 1):
                h = goal - a
                if not 0 <= h < depth:
                    continue
                lanes = pl.ds(((a + 1) * 3 + b + 1) * cin, cin)
                main = zed[i, h, 0:band, lanes]
                inner = main if inner is None else inner + main
                if b != 0:
                    line = zed[i, h, pl.ds(band, TILE), lanes]
                    enter = line if enter is None else enter + line
            if b == 0:
                total = inner
            elif b == 1:
                entering = jnp.where(c == 1, enter[TILE - 1 : TILE], 0.0)
                total = total + shifted(inner, 1, entering)
            else:
                entering = jnp.where(c == 0, enter[0:1], 0.0)
                total = total + shifted(inner, -1, entering)
        return total

    def from_above(i):
        @pl.when(has_up)
        def _():
            tile_down(i).wait_recv()
            down(i).wait_recv()

        lay(0, i)

    def from_below(i):
        @pl.when(has_down)
        def _():
            tile_up(i).wait_recv()
            up(i).wait_recv()

        lay(depth + 1, i)

    def give(side, goal, allowed):
        for i in (0, 1):
            part_out[side, i] = gathered(i, goal).astype(BF16)

            @pl.when(allowed)
            def _():
                part_copy(side, i).start()

    def entering(h, i):
        if h == 0:
            from_above(i)
        if h == depth - 1:
            from_below(i)

    for h in range(depth):
        process(h, functools.partial(entering, h))
        if h == 0:
            give(0, -1, has_up)
            if rounds > 1:
                hear_word(1)
            if rounds > 2:
                spread_word(2)
        if h < depth - 1:
            for k in range(3):
                term = weight_term(h, k)
                early[k] = term if h == 0 else early[k] + term
    give(1, depth, has_down)

    for k in range(2, rounds):
        hear_word(k)
        if k + 1 < rounds:
            spread_word(k + 1)

    scale = 1.0 / math.sqrt(2 * depth * band * group)

    def pair_copy(k):
        return remote(pair_out.at[k, other], pair_in.at[k], pair_send.at[k], pair_recv.at[k], r, other)

    def chunk_copy(k, i):
        target = lax.rem(r + i, rows)
        return remote(
            chunk.at[k, target], landed.at[k, i], chunk_send.at[k, i], chunk_recv.at[k, i], target, c
        )

    for k in range(3):
        total = weight_term(depth - 1, k)
        if depth > 1:
            total = total + early[k]
        total = total * scale
        for s in range(rows):
            for col in range(cols):
                start = (s * cols + col) * quota
                piece = total[start : start + quota]
                acc[k, col, s] = piece
                pair_out[k, col, s] = piece.astype(BF16)
        pair_copy(k).start()
    for k in range(3):
        pair_copy(k).wait_recv()
        for s in range(rows):
            both = acc[k, c, s] + pair_in[k, s].astype(F32)
            acc[k, c, s] = both
            chunk[k, s] = both.astype(BF16)

        def start_chunk(i, carry):
            chunk_copy(k, i).start()
            return carry

        lax.fori_loop(1, rows, start_chunk, 0)

    outs = (gl_buf, gr_buf)

    def store(i, goal):
        return pltpu.make_async_copy(outs[i].at[goal], (gl_out, gr_out)[i].at[goal], store_sem.at[i, goal])

    def put(goal):
        for i in (0, 1):
            total = gathered(i, goal)
            if goal == 0:
                total = total + jnp.where(has_up, part_in[0, i].astype(F32), 0.0)
            if goal == depth - 1:
                total = total + jnp.where(has_down, part_in[1, i].astype(F32), 0.0)
            outs[i][goal] = total.astype(BF16)
            store(i, goal).start()

    @pl.when(has_down)
    def _():
        for i in (0, 1):
            part_copy(0, i).wait_recv()

    for goal in range(depth - 1, 0, -1):
        put(goal)

    @pl.when(has_up)
    def _():
        for i in (0, 1):
            part_copy(1, i).wait_recv()

    put(0)

    def last_copy(k):
        return remote(whole.at[k, c], whole.at[k, c], whole_send.at[k], whole_recv.at[k], r, other)

    for k in range(3):

        def wait_chunk(i, carry):
            chunk_copy(k, i).wait_recv()
            return carry

        def add_chunk(i, total):
            return total + landed[k, i].astype(F32)

        lax.fori_loop(1, rows, wait_chunk, 0)
        whole[k, c] = lax.fori_loop(1, rows, add_chunk, acc[k, c, r])
        last_copy(k).start()
    for k in range(3):
        last_copy(k).wait_recv()
        for col in range(cols):
            wg_buf[pl.ds(col * quota, quota), pl.ds(k * 3 * cin, 3 * cin)] = whole[k, col]

    whole_store = pltpu.make_async_copy(wg_buf, wg_out, load_sem.at[0])
    whole_store.start()
    for k in range(3):
        last_copy(k).wait_send()
        pair_copy(k).wait_send()

        def drain(i, carry):
            chunk_copy(k, i).wait_send()
            return carry

        lax.fori_loop(1, rows, drain, 0)
    for i in (0, 1):
        tile_mid(i).wait_send()
    for h in range(depth):
        edge_copy(h).wait_send()

    @pl.when(has_down)
    def _():
        for i in (0, 1):
            part_copy(1, i).wait_send()

    @pl.when(has_up)
    def _():
        for i in (0, 1):
            tile_up(i).wait_send()
            up(i).wait_send()
            part_copy(0, i).wait_send()

    @pl.when(c == 0)
    def _():
        for h in range(depth):
            ext_copy(h).wait_send()

    @pl.when(c == 1)
    def _():
        for h in range(depth):
            ret_copy(h).wait_send()

    for i in (0, 1):
        for goal in range(depth):
            store(i, goal).wait()
    whole_store.wait()


def hand_over(a, b, w, a_out, b_out, w_out, a_mid, b_mid, w_mid, sem_in, sem_out):
    into = [
        pltpu.make_async_copy(src, mid, sem_in.at[k])
        for k, (src, mid) in enumerate(((a, a_mid), (b, b_mid), (w, w_mid)))
    ]
    out = [
        pltpu.make_async_copy(mid, dst, sem_out.at[k])
        for k, (mid, dst) in enumerate(((a_mid, a_out), (b_mid, b_out), (w_mid, w_out)))
    ]
    for copy in into:
        copy.start()
    for first, second in zip(into, out):
        first.wait()
        second.start()
    for copy in out:
        copy.wait()


def on_device(rows, cols, left, right, weight, l0, l1, l2, l3):
    depth, band, cin = left.shape
    taps, features = weight.shape
    reach = l0.shape[2]
    blocks = band // reach
    quota = features // (rows * cols)
    third = taps // 3
    l2 = jnp.swapaxes(l2, 1, 2)
    l3 = jnp.swapaxes(l3, 1, 2)
    dma = pltpu.SemaphoreType.DMA
    results = pl.pallas_call(
        functools.partial(kernel, rows, cols),
        out_shape=(
            jax.ShapeDtypeStruct(left.shape, BF16),
            jax.ShapeDtypeStruct(right.shape, BF16),
            jax.ShapeDtypeStruct((features // rows, taps), F32),
        ),
        in_specs=[pl.BlockSpec(memory_space=pl.ANY)] * 7,
        out_specs=(pl.BlockSpec(memory_space=pl.ANY),) * 3,
        scratch_shapes=[
            *(pltpu.VMEM(x.shape, BF16) for x in (left, right, left, right)),
            pltpu.VMEM((features // rows, taps), F32),
            *(pltpu.VMEM(x.shape, BF16) for x in (weight, l0, l1, l2, l3)),
            pltpu.VMEM((2, 2, band, cin), BF16),
            pltpu.VMEM((2, depth + 2, TILE, cin), BF16),
            pltpu.VMEM((depth, blocks, reach, 2 * reach), BF16),
            pltpu.VMEM((2, depth, band, taps), BF16),
            pltpu.VMEM((band, features), BF16),
            pltpu.VMEM((depth, reach + band, features), BF16),
            pltpu.VMEM((depth, reach, features), BF16),
            pltpu.VMEM((depth, reach, features), BF16),
            pltpu.VMEM((2, depth, band, features), BF16),
            pltpu.VMEM((2, depth, TILE, features), BF16),
            pltpu.VMEM((2, depth, band + TILE, taps), F32),
            pltpu.VMEM((2, 2, band, cin), BF16),
            pltpu.VMEM((2, 2, band, cin), BF16),
            pltpu.VMEM((3, cols, rows, quota, third), F32),
            pltpu.VMEM((3, features, third), F32),
            pltpu.VMEM((3, cols, rows, quota, third), BF16),
            pltpu.VMEM((3, rows, quota, third), BF16),
            pltpu.VMEM((3, rows, quota, third), BF16),
            pltpu.VMEM((3, rows, quota, third), BF16),
            pltpu.VMEM((3, cols, quota, third), F32),
            dma((2, 2)), dma((2, 2)), dma((3, 2)), dma((3, 2)),
            dma((depth,)), dma((depth,)), dma((depth,)), dma((depth,)),
            dma((depth,)), dma((depth,)), dma((2, 2)), dma((2, 2)),
            dma((3,)), dma((3,)), dma((3, rows)), dma((3, rows)), dma((3,)), dma((3,)), dma((7,)),
            dma((2, depth)), pltpu.SemaphoreType.REGULAR(((rows - 1).bit_length(), 2)),
        ],
        compiler_params=pltpu.CompilerParams(
            collective_id=0, has_side_effects=True, vmem_limit_bytes=60 * 1024 * 1024
        ),
        name="stereo_backward",
    )(left, right, weight, l0, l1, l2, l3)
    hbm = pl.BlockSpec(memory_space=pl.ANY)
    shapes = tuple(jax.ShapeDtypeStruct(x.shape, x.dtype) for x in results)
    return pl.pallas_call(
        hand_over,
        out_shape=shapes,
        in_specs=[hbm] * 3,
        out_specs=(hbm,) * 3,
        scratch_shapes=[*(pltpu.VMEM(x.shape, x.dtype) for x in results), dma((3,)), dma((3,))],
        name="hand_over",
    )(*results)


def solution(mesh):
    banded = P(("pairs", "rows"), "cols", None)
    return jax.shard_map(
        functools.partial(on_device, mesh.shape["rows"], mesh.shape["cols"]),
        mesh=mesh,
        in_specs=(banded, banded, P(), banded, banded, banded, banded),
        out_specs=(banded, banded, P(("pairs", "rows"), None)),
        check_vma=False,
    )
```

```python
import functools
import math

import jax
import jax.numpy as jnp
from jax import lax
from jax.experimental import pallas as pl
from jax.experimental.pallas import tpu as pltpu
from jax.sharding import PartitionSpec as P

F32 = jnp.float32
BF16 = jnp.bfloat16
TILE = 16


def remote(src, dst, send, recv, row, col):
    return pltpu.make_async_remote_copy(
        src_ref=src,
        dst_ref=dst,
        send_sem=send,
        recv_sem=recv,
        device_id={"rows": row, "cols": col},
        device_id_type=pl.DeviceIdType.MESH,
    )


def matmul(a, b, dims):
    return lax.dot_general(a, b, (dims, ((), ())), preferred_element_type=F32)


def expansion(levels, reach, factor):
    source = lax.broadcasted_iota(jnp.int32, (levels, reach), 0)
    target = (reach - 1) - lax.broadcasted_iota(jnp.int32, (levels, reach), 1)
    bits = factor.bit_length() - 1
    hit = lax.shift_right_logical(target, jnp.int32(bits)) == source
    return jnp.where(hit, 1.0 / factor, 0.0).astype(BF16)


def kernel(
    rows, cols, left_hbm, right_hbm, weight_hbm, l0_hbm, l1_hbm, l2_hbm, l3_hbm, gl_out, gr_out, wg_out,
    left, right, gl_buf, gr_buf, wg_buf, weight, l0, l1, l2, l3, halo_row, halo_col, band_m, patch, left_feat, right_ext, ret_out, ret_in,
    grad, grad_edge, zed, part_out, part_in, own_conv, acc, early, pair_out, pair_in, cross_out, cross_in, chunk, landed, whole,
    row_send, row_recv, col_send, col_recv, ext_send, ext_recv, ret_send, ret_recv,
    edge_send, edge_recv, part_send, part_recv, pair_send, pair_recv, cross_send, cross_recv, chunk_send, chunk_recv, whole_send, whole_recv, load_sem, store_sem, known,
):
    depth, band, cin = left.shape
    features = weight.shape[1]
    reach = l0.shape[2]
    blocks = band // reach
    quota = features // (rows * cols)
    r = lax.axis_index("rows")
    c = lax.axis_index("cols")
    other = 1 - c
    images = (left, right)
    sources = (left_hbm, right_hbm)
    group = rows * cols
    has_up = r > 0
    has_down = r < rows - 1

    barrier = pltpu.get_barrier_semaphore()

    def tell(semaphore, row, col):
        pl.semaphore_signal(
            semaphore, inc=1, device_id={"rows": row, "cols": col}, device_id_type=pl.DeviceIdType.MESH
        )

    tell(barrier, r, other)

    @pl.when(has_up)
    def _():
        for col in (c, other):
            tell(barrier, r - 1, col)

    @pl.when(has_down)
    def _():
        for col in (c, other):
            tell(barrier, r + 1, col)

    loads = [
        pltpu.make_async_copy(src, dst, load_sem.at[k])
        for k, (src, dst) in enumerate(
            (
                (l0_hbm, l0), (l1_hbm, l1), (l2_hbm, l2), (l3_hbm, l3),
                (right_hbm, right), (left_hbm, left), (weight_hbm, weight),
            )
        )
    ]
    for load in loads:
        load.start()
    pl.semaphore_wait(barrier, 1 + 2 * has_up.astype(jnp.int32) + 2 * has_down.astype(jnp.int32))

    rounds = (rows - 1).bit_length()

    def spread_word(k):
        @pl.when(r >= 2**k)
        def _():
            tell(known.at[k, 1], r - 2**k, c)

        @pl.when(r + 2**k < rows)
        def _():
            tell(known.at[k, 0], r + 2**k, c)

    def hear_word(k):
        @pl.when(r >= 2**k)
        def _():
            pl.semaphore_wait(known.at[k, 0], 1)

        @pl.when(r + 2**k < rows)
        def _():
            pl.semaphore_wait(known.at[k, 1], 1)

    near = pl.multiple_of(other * (band - TILE), TILE)

    def down(i):
        return remote(sources[i].at[depth - 1], halo_row.at[0, i], row_send.at[0, i], row_recv.at[0, i], r + 1, c)

    def up(i):
        return remote(sources[i].at[0], halo_row.at[1, i], row_send.at[1, i], row_recv.at[1, i], r - 1, c)

    def tile_mid(i):
        return remote(
            sources[i].at[:, pl.ds(near, TILE)], halo_col.at[i, pl.ds(1, depth)],
            col_send.at[0, i], col_recv.at[0, i], r, other,
        )

    def tile_down(i):
        return remote(
            sources[i].at[depth - 1, pl.ds(near, TILE)], halo_col.at[i, 0],
            col_send.at[1, i], col_recv.at[1, i], r + 1, other,
        )

    def tile_up(i):
        return remote(
            sources[i].at[0, pl.ds(near, TILE)], halo_col.at[i, depth + 1],
            col_send.at[2, i], col_recv.at[2, i], r - 1, other,
        )

    for i in (1, 0):
        tile_mid(i).start()

    @pl.when(has_down)
    def _():
        for i in (1, 0):
            tile_down(i).start()
            down(i).start()

    spread_word(0)

    @pl.when(r == 0)
    def _():
        halo_row[0] = jnp.zeros_like(halo_row[0])
        for i in (0, 1):
            halo_col[i, 0] = jnp.zeros_like(halo_col[i, 0])

    @pl.when(r == rows - 1)
    def _():
        halo_row[1] = jnp.zeros_like(halo_row[1])
        for i in (0, 1):
            halo_col[i, depth + 1] = jnp.zeros_like(halo_col[i, depth + 1])

    spread = [expansion(count, reach, reach // count) for count in (reach, l1.shape[2], l2.shape[1], l3.shape[1])]
    for load in loads[:4]:
        load.wait()
    for h in range(depth):
        for s in range(blocks):
            at = pl.ds(s * reach, reach)
            total = matmul(l0[h, at], spread[0], ((1,), (0,)))
            total = total + matmul(l1[h, at], spread[1], ((1,), (0,)))
            for level, way in zip((l2, l3), spread[2:]):
                total = total + matmul(level[h, :, at], way, ((0,), (0,)))
            total = total.astype(BF16).astype(F32)
            wide = jnp.concatenate([total, jnp.zeros_like(total)], axis=1)
            band_m[h, s] = pltpu.roll(wide, 1, 1, stride=1, stride_axis=0).astype(BF16)

    place = lax.broadcasted_iota(jnp.int32, (band, cin), 0)

    def shifted(x, by, edge):
        if by == 1:
            return jnp.where(place == 0, edge, pltpu.roll(x, 1, 0))
        return jnp.where(place == band - 1, edge, pltpu.roll(x, band - 1, 0))

    def lay(framed, i):
        if framed == 0:
            base = halo_row[0, i]
        elif framed == depth + 1:
            base = halo_row[1, i]
        else:
            base = images[i][framed - 1]
        tile = halo_col[i, framed].astype(F32)
        zero = jnp.zeros((1, cin), F32)
        enter_left = jnp.where(c == 0, zero, tile[TILE - 1 : TILE])
        enter_right = jnp.where(c == 0, tile[0:1], zero)
        wide = base.astype(F32)
        three = (
            shifted(wide, 1, enter_left).astype(BF16),
            base,
            shifted(wide, -1, enter_right).astype(BF16),
        )
        for row_tap in range(3):
            h = framed - row_tap
            if 0 <= h < depth:
                for k in range(3):
                    patch[i, h, :, pl.ds((row_tap * 3 + k) * cin, cin)] = three[k]

    inverse = 1.0 / math.sqrt(features)

    def ext_copy(h):
        return remote(
            right_ext.at[h, pl.ds(band, reach)], right_ext.at[h, pl.ds(0, reach)],
            ext_send.at[h], ext_recv.at[h], r, other,
        )

    def ret_copy(h):
        return remote(ret_out.at[h], ret_in.at[h], ret_send.at[h], ret_recv.at[h], r, other)

    def edge_copy(h, i):
        return remote(
            grad.at[i, h, pl.ds(near, TILE)], grad_edge.at[i, h], edge_send.at[i, h], edge_recv.at[i, h], r, other
        )

    def part_copy(side, i):
        target = r - 1 if side == 0 else r + 1
        return remote(
            part_out.at[side, i], part_in.at[1 - side, i], part_send.at[side, i], part_recv.at[1 - side, i],
            target, c,
        )

    @pl.when(c == 0)
    def _():
        right_ext[:, 0:reach] = jnp.zeros((depth, reach, features), BF16)

    def own_taps(h):
        return (0 if h > 0 else 1), (3 if h < depth - 1 else 2)

    def convolve(i, h, first, last):
        lanes = pl.ds(first * 3 * cin, (last - first) * 3 * cin)
        return matmul(patch[i, h, :, lanes], weight[lanes], ((1,), (0,)))

    def feature(i, h):
        first, last = own_taps(h)
        total = own_conv[i, h]
        if first > 0:
            total = total + convolve(i, h, 0, first)
        if last < 3:
            total = total + convolve(i, h, last, 3)
        return total.astype(BF16)

    def weight_term(i, h):
        return matmul(grad[i, h], patch[i, h], ((0,), (0,)))

    def spread_grad(i, h):
        zed[i, h, 0:band] = matmul(grad[i, h], weight[...], ((1,), (1,)))

    def spread_edge(i, h):
        edge_copy(h, i).wait_recv()
        zed[i, h, pl.ds(band, TILE)] = matmul(grad_edge[i, h], weight[...], ((1,), (1,)))

    def left_chain(h):
        right_ext[h, pl.ds(reach, band)] = feature(1, h)

        @pl.when(c == 0)
        def _():
            ext_copy(h).start()

        for s in range(blocks - 1, -1, -1):
            if s == 0:

                @pl.when(c == 1)
                def _():
                    ext_copy(h).wait_recv()

            window = right_ext[h, pl.ds(s * reach, 2 * reach)]
            out = matmul(band_m[h, s], window, ((1,), (0,)))
            grad[0, h, pl.ds(s * reach, reach)] = (out * inverse).astype(BF16)
        edge_copy(h, 0).start()
        spread_grad(0, h)
        spread_edge(0, h)

    def right_chain(h):
        left_feat[...] = feature(0, h)
        pending = None
        for s in range(blocks):
            both = matmul(band_m[h, s], left_feat[pl.ds(s * reach, reach)], ((0,), (0,)))
            head = both[:reach]
            if s == 0:
                ret_out[h] = head.astype(BF16)

                @pl.when(c == 1)
                def _():
                    ret_copy(h).start()
            else:
                grad[1, h, pl.ds((s - 1) * reach, reach)] = ((pending + head) * inverse).astype(BF16)
            pending = both[reach:]

        if h == 0:
            early[...] = weight_term(0, h)
        else:
            early[...] += weight_term(0, h)

        @pl.when(c == 0)
        def _():
            ret_copy(h).wait_recv()

        came = jnp.where(c == 0, ret_in[h].astype(F32), 0.0)
        grad[1, h, pl.ds(band - reach, reach)] = ((pending + came) * inverse).astype(BF16)
        edge_copy(h, 1).start()

    def gathered(i, goal):
        total = None
        for b in (0, 1, -1):
            inner = None
            enter = None
            for a in (-1, 0, 1):
                h = goal - a
                if not 0 <= h < depth:
                    continue
                lanes = pl.ds(((a + 1) * 3 + b + 1) * cin, cin)
                main = zed[i, h, 0:band, lanes]
                inner = main if inner is None else inner + main
                if b != 0:
                    line = zed[i, h, pl.ds(band, TILE), lanes]
                    enter = line if enter is None else enter + line
            if b == 0:
                total = inner
            elif b == 1:
                entering = jnp.where(c == 1, enter[TILE - 1 : TILE], 0.0)
                total = total + shifted(inner, 1, entering)
            else:
                entering = jnp.where(c == 0, enter[0:1], 0.0)
                total = total + shifted(inner, -1, entering)
        return total

    for load in loads[4:]:
        load.wait()
    for i in (1, 0):
        tile_mid(i).wait_recv()
        for framed in range(1, depth + 1):
            lay(framed, i)
    for i in (1, 0):
        for h in range(depth):
            own_conv[i, h] = convolve(i, h, *own_taps(h))

    @pl.when(has_down)
    def _():
        for i in (1, 0):
            tile_down(i).wait_send()
            down(i).wait_send()

    @pl.when(has_up)
    def _():
        for i in (1, 0):
            tile_up(i).start()
            up(i).start()

    hear_word(0)
    if rounds > 1:
        spread_word(1)

    def from_above(i):
        @pl.when(has_up)
        def _():
            tile_down(i).wait_recv()
            down(i).wait_recv()

        lay(0, i)

    def from_below(i):
        @pl.when(has_down)
        def _():
            tile_up(i).wait_recv()
            up(i).wait_recv()

        lay(depth + 1, i)

    def give(side, goal, allowed, i):
        part_out[side, i] = gathered(i, goal).astype(BF16)

        @pl.when(allowed)
        def _():
            part_copy(side, i).start()

    def entering(h, i):
        if h == 0:
            from_above(i)
        if h == depth - 1:
            from_below(i)

    def pair_copy(k):
        return remote(pair_out.at[k, other], pair_in.at[k], pair_send.at[k], pair_recv.at[k], r, other)

    scale = 1.0 / math.sqrt(2 * depth * band * group)
    for h in range(depth):
        entering(h, 1)
        left_chain(h)
        entering(h, 0)
        right_chain(h)
        if h < depth - 1:
            early[...] += weight_term(1, h)
        else:
            for k in range(3):
                lanes = pl.ds(k * 3 * cin, 3 * cin)
                total = matmul(grad[1, h], patch[1, h, :, lanes], ((0,), (0,)))
                total = (early[:, lanes] + total) * scale
                for s in range(rows):
                    for col in range(cols):
                        start = (s * cols + col) * quota
                        piece = total[start : start + quota]
                        acc[k, col, s % 2, s // 2] = piece
                        pair_out[k, col, s % 2, s // 2] = piece.astype(BF16)
                pair_copy(k).start()
        spread_grad(1, h)
        spread_edge(1, h)
        if h == 0:
            for i in (0, 1):
                give(0, -1, has_up, i)
            if rounds > 1:
                hear_word(1)
            if rounds > 2:
                spread_word(2)
    for k in range(2, rounds):
        hear_word(k)
        if k + 1 < rounds:
            spread_word(k + 1)

    half = rows // 2
    place_in_half = r // 2
    parity = lax.rem(r, 2)
    across = r + 1 - 2 * parity

    def cross_copy(k):
        return remote(cross_out.at[k], cross_in.at[k], cross_send.at[k], cross_recv.at[k], across, c)

    def chunk_copy(k, i):
        goal = lax.rem(place_in_half + i, half)
        return remote(
            chunk.at[k, goal], landed.at[k, i], chunk_send.at[k, i], chunk_recv.at[k, i], 2 * goal + parity, c
        )

    for k in range(3):
        pair_copy(k).wait_recv()
        cross_out[k] = (acc[k, c, 1 - parity] + pair_in[k, 1 - parity].astype(F32)).astype(BF16)
        cross_copy(k).start()
        acc[k, c, parity] += pair_in[k, parity].astype(F32)


    outs = (gl_buf, gr_buf)

    def store(i, goal):
        return pltpu.make_async_copy(outs[i].at[goal], (gl_out, gr_out)[i].at[goal], store_sem.at[i, goal])

    def put(goal):
        for i in (0, 1):
            total = gathered(i, goal)
            if goal == 0:
                total = total + jnp.where(has_up, part_in[0, i].astype(F32), 0.0)
            if goal == depth - 1:
                total = total + jnp.where(has_down, part_in[1, i].astype(F32), 0.0)
            outs[i][goal] = total.astype(BF16)
            store(i, goal).start()

    def last_copy(k):
        return remote(whole.at[k, c], whole.at[k, c], whole_send.at[k], whole_recv.at[k], r, other)

    for k in range(3):
        cross_copy(k).wait_recv()
        total = acc[k, c, parity] + cross_in[k].astype(F32)
        acc[k, c, parity] = total
        chunk[k] = total.astype(BF16)

        def start_chunk(i, carry):
            chunk_copy(k, i).start()
            return carry

        lax.fori_loop(1, half, start_chunk, 0)

    for i in (0, 1):
        give(1, depth, has_down, i)

    @pl.when(has_down)
    def _():
        for i in (0, 1):
            part_copy(0, i).wait_recv()

    for goal in range(depth - 1, 0, -1):
        put(goal)

    for k in range(3):

        def wait_chunk(i, carry):
            chunk_copy(k, i).wait_recv()
            return carry

        def add_chunk(i, total):
            return total + landed[k, i].astype(F32)

        lax.fori_loop(1, half, wait_chunk, 0)
        whole[k, c] = lax.fori_loop(1, half, add_chunk, acc[k, c, parity, place_in_half])
        last_copy(k).start()

    @pl.when(has_up)
    def _():
        for i in (0, 1):
            part_copy(1, i).wait_recv()

    put(0)

    for k in range(3):
        last_copy(k).wait_recv()
        for col in range(cols):
            wg_buf[pl.ds(col * quota, quota), pl.ds(k * 3 * cin, 3 * cin)] = whole[k, col]

    whole_store = pltpu.make_async_copy(wg_buf, wg_out, load_sem.at[0])
    whole_store.start()
    for k in range(3):
        last_copy(k).wait_send()
        pair_copy(k).wait_send()
        cross_copy(k).wait_send()

        def drain(i, carry):
            chunk_copy(k, i).wait_send()
            return carry

        lax.fori_loop(1, half, drain, 0)
    for i in (0, 1):
        tile_mid(i).wait_send()
    for h in range(depth):
        for i in (0, 1):
            edge_copy(h, i).wait_send()

    @pl.when(has_down)
    def _():
        for i in (0, 1):
            part_copy(1, i).wait_send()

    @pl.when(has_up)
    def _():
        for i in (0, 1):
            tile_up(i).wait_send()
            up(i).wait_send()
            part_copy(0, i).wait_send()

    @pl.when(c == 0)
    def _():
        for h in range(depth):
            ext_copy(h).wait_send()

    @pl.when(c == 1)
    def _():
        for h in range(depth):
            ret_copy(h).wait_send()

    for i in (0, 1):
        for goal in range(depth):
            store(i, goal).wait()
    whole_store.wait()


def hand_over(a, b, w, a_out, b_out, w_out, a_mid, b_mid, w_mid, sem_in, sem_out):
    into = [
        pltpu.make_async_copy(src, mid, sem_in.at[k])
        for k, (src, mid) in enumerate(((a, a_mid), (b, b_mid), (w, w_mid)))
    ]
    out = [
        pltpu.make_async_copy(mid, dst, sem_out.at[k])
        for k, (mid, dst) in enumerate(((a_mid, a_out), (b_mid, b_out), (w_mid, w_out)))
    ]
    for copy in into:
        copy.start()
    for first, second in zip(into, out):
        first.wait()
        second.start()
    for copy in out:
        copy.wait()


def on_device(rows, cols, left, right, weight, l0, l1, l2, l3):
    depth, band, cin = left.shape
    taps, features = weight.shape
    reach = l0.shape[2]
    blocks = band // reach
    quota = features // (rows * cols)
    third = taps // 3
    l2 = jnp.swapaxes(l2, 1, 2)
    l3 = jnp.swapaxes(l3, 1, 2)
    dma = pltpu.SemaphoreType.DMA
    results = pl.pallas_call(
        functools.partial(kernel, rows, cols),
        out_shape=(
            jax.ShapeDtypeStruct(left.shape, BF16),
            jax.ShapeDtypeStruct(right.shape, BF16),
            jax.ShapeDtypeStruct((features // rows, taps), F32),
        ),
        in_specs=[pl.BlockSpec(memory_space=pl.ANY)] * 7,
        out_specs=(pl.BlockSpec(memory_space=pl.ANY),) * 3,
        scratch_shapes=[
            *(pltpu.VMEM(x.shape, BF16) for x in (left, right, left, right)),
            pltpu.VMEM((features // rows, taps), F32),
            *(pltpu.VMEM(x.shape, BF16) for x in (weight, l0, l1, l2, l3)),
            pltpu.VMEM((2, 2, band, cin), BF16),
            pltpu.VMEM((2, depth + 2, TILE, cin), BF16),
            pltpu.VMEM((depth, blocks, reach, 2 * reach), BF16),
            pltpu.VMEM((2, depth, band, taps), BF16),
            pltpu.VMEM((band, features), BF16),
            pltpu.VMEM((depth, reach + band, features), BF16),
            pltpu.VMEM((depth, reach, features), BF16),
            pltpu.VMEM((depth, reach, features), BF16),
            pltpu.VMEM((2, depth, band, features), BF16),
            pltpu.VMEM((2, depth, TILE, features), BF16),
            pltpu.VMEM((2, depth, band + TILE, taps), F32),
            pltpu.VMEM((2, 2, band, cin), BF16),
            pltpu.VMEM((2, 2, band, cin), BF16),
            pltpu.VMEM((2, depth, band, features), F32),
            pltpu.VMEM((3, cols, 2, rows // 2, quota, third), F32),
            pltpu.VMEM((features, taps), F32),
            pltpu.VMEM((3, cols, 2, rows // 2, quota, third), BF16),
            pltpu.VMEM((3, 2, rows // 2, quota, third), BF16),
            *(pltpu.VMEM((3, rows // 2, quota, third), BF16) for _ in range(4)),
            pltpu.VMEM((3, cols, quota, third), F32),
            dma((2, 2)), dma((2, 2)), dma((3, 2)), dma((3, 2)),
            dma((depth,)), dma((depth,)), dma((depth,)), dma((depth,)),
            dma((2, depth)), dma((2, depth)), dma((2, 2)), dma((2, 2)),
            dma((3,)), dma((3,)), dma((3,)), dma((3,)), dma((3, rows // 2)), dma((3, rows // 2)), dma((3,)), dma((3,)), dma((7,)),
            dma((2, depth)), pltpu.SemaphoreType.REGULAR(((rows - 1).bit_length(), 2)),
        ],
        compiler_params=pltpu.CompilerParams(
            collective_id=0, has_side_effects=True, vmem_limit_bytes=60 * 1024 * 1024
        ),
        name="stereo_backward",
    )(left, right, weight, l0, l1, l2, l3)
    hbm = pl.BlockSpec(memory_space=pl.ANY)
    shapes = tuple(jax.ShapeDtypeStruct(x.shape, x.dtype) for x in results)
    return pl.pallas_call(
        hand_over,
        out_shape=shapes,
        in_specs=[hbm] * 3,
        out_specs=(hbm,) * 3,
        scratch_shapes=[*(pltpu.VMEM(x.shape, x.dtype) for x in results), dma((3,)), dma((3,))],
        name="hand_over",
    )(*results)


def solution(mesh):
    banded = P(("pairs", "rows"), "cols", None)
    return jax.shard_map(
        functools.partial(on_device, mesh.shape["rows"], mesh.shape["cols"]),
        mesh=mesh,
        in_specs=(banded, banded, P(), banded, banded, banded, banded),
        out_specs=(banded, banded, P(("pairs", "rows"), None)),
        check_vma=False,
    )
```

```python
import functools
import math

import jax
import jax.numpy as jnp
from jax import lax
from jax.experimental import pallas as pl
from jax.experimental.pallas import tpu as pltpu
from jax.sharding import PartitionSpec as P

F32 = jnp.float32
BF16 = jnp.bfloat16
TILE = 16


def remote(src, dst, send, recv, row, col):
    return pltpu.make_async_remote_copy(
        src_ref=src,
        dst_ref=dst,
        send_sem=send,
        recv_sem=recv,
        device_id={"rows": row, "cols": col},
        device_id_type=pl.DeviceIdType.MESH,
    )


def matmul(a, b, dims):
    return lax.dot_general(a, b, (dims, ((), ())), preferred_element_type=F32)


def expansion(levels, reach, factor):
    source = lax.broadcasted_iota(jnp.int32, (levels, reach), 0)
    target = (reach - 1) - lax.broadcasted_iota(jnp.int32, (levels, reach), 1)
    bits = factor.bit_length() - 1
    hit = lax.shift_right_logical(target, jnp.int32(bits)) == source
    return jnp.where(hit, 1.0 / factor, 0.0).astype(BF16)


def kernel(
    rows, cols, left_hbm, right_hbm, weight_hbm, l0_hbm, l1_hbm, l2_hbm, l3_hbm, gl_out, gr_out, wg_out,
    left, right, gl_buf, gr_buf, wg_buf, weight, l0, l1, l2, l3, halo_row, halo_col, band_m, patch, left_feat, right_ext, ret_out, ret_in,
    grad, grad_edge, zed, part_out, part_in, own_conv, acc, early, pair_out, pair_in, cross_out, cross_in, chunk, landed, whole,
    row_send, row_recv, col_send, col_recv, ext_send, ext_recv, ret_send, ret_recv,
    edge_send, edge_recv, part_send, part_recv, pair_send, pair_recv, cross_send, cross_recv, chunk_send, chunk_recv, whole_send, whole_recv, load_sem, store_sem, known,
):
    depth, band, cin = left.shape
    features = weight.shape[1]
    reach = l0.shape[2]
    blocks = band // reach
    quota = features // (rows * cols)
    r = lax.axis_index("rows")
    c = lax.axis_index("cols")
    other = 1 - c
    images = (left, right)
    sources = (left_hbm, right_hbm)
    group = rows * cols
    has_up = r > 0
    has_down = r < rows - 1

    barrier = pltpu.get_barrier_semaphore()

    def tell(semaphore, row, col):
        pl.semaphore_signal(
            semaphore, inc=1, device_id={"rows": row, "cols": col}, device_id_type=pl.DeviceIdType.MESH
        )

    tell(barrier, r, other)

    @pl.when(has_up)
    def _():
        for col in (c, other):
            tell(barrier, r - 1, col)

    @pl.when(has_down)
    def _():
        for col in (c, other):
            tell(barrier, r + 1, col)

    loads = [
        pltpu.make_async_copy(src, dst, load_sem.at[k])
        for k, (src, dst) in enumerate(
            (
                (l0_hbm, l0), (l1_hbm, l1), (l2_hbm, l2), (l3_hbm, l3),
                (right_hbm, right), (left_hbm, left), (weight_hbm, weight),
            )
        )
    ]
    for load in loads:
        load.start()
    pl.semaphore_wait(barrier, 1 + 2 * has_up.astype(jnp.int32) + 2 * has_down.astype(jnp.int32))

    rounds = (rows - 1).bit_length()

    def spread_word(k):
        @pl.when(r >= 2**k)
        def _():
            tell(known.at[k, 1], r - 2**k, c)

        @pl.when(r + 2**k < rows)
        def _():
            tell(known.at[k, 0], r + 2**k, c)

    def hear_word(k):
        @pl.when(r >= 2**k)
        def _():
            pl.semaphore_wait(known.at[k, 0], 1)

        @pl.when(r + 2**k < rows)
        def _():
            pl.semaphore_wait(known.at[k, 1], 1)

    near = pl.multiple_of(other * (band - TILE), TILE)

    def down(i):
        return remote(sources[i].at[depth - 1], halo_row.at[0, i], row_send.at[0, i], row_recv.at[0, i], r + 1, c)

    def up(i):
        return remote(sources[i].at[0], halo_row.at[1, i], row_send.at[1, i], row_recv.at[1, i], r - 1, c)

    def tile_mid(i):
        return remote(
            sources[i].at[:, pl.ds(near, TILE)], halo_col.at[i, pl.ds(1, depth)],
            col_send.at[0, i], col_recv.at[0, i], r, other,
        )

    def tile_down(i):
        return remote(
            sources[i].at[depth - 1, pl.ds(near, TILE)], halo_col.at[i, 0],
            col_send.at[1, i], col_recv.at[1, i], r + 1, other,
        )

    def tile_up(i):
        return remote(
            sources[i].at[0, pl.ds(near, TILE)], halo_col.at[i, depth + 1],
            col_send.at[2, i], col_recv.at[2, i], r - 1, other,
        )

    for i in (1, 0):
        tile_mid(i).start()

    @pl.when(has_down)
    def _():
        for i in (1, 0):
            tile_down(i).start()
            down(i).start()

    spread_word(0)

    @pl.when(r == 0)
    def _():
        halo_row[0] = jnp.zeros_like(halo_row[0])
        for i in (0, 1):
            halo_col[i, 0] = jnp.zeros_like(halo_col[i, 0])

    @pl.when(r == rows - 1)
    def _():
        halo_row[1] = jnp.zeros_like(halo_row[1])
        for i in (0, 1):
            halo_col[i, depth + 1] = jnp.zeros_like(halo_col[i, depth + 1])

    spread = [expansion(count, reach, reach // count) for count in (reach, l1.shape[2], l2.shape[1], l3.shape[1])]
    for load in loads[:4]:
        load.wait()
    for h in range(depth):
        for s in range(blocks):
            at = pl.ds(s * reach, reach)
            total = matmul(l0[h, at], spread[0], ((1,), (0,)))
            total = total + matmul(l1[h, at], spread[1], ((1,), (0,)))
            for level, way in zip((l2, l3), spread[2:]):
                total = total + matmul(level[h, :, at], way, ((0,), (0,)))
            total = total.astype(BF16).astype(F32)
            wide = jnp.concatenate([total, jnp.zeros_like(total)], axis=1)
            band_m[h, s] = pltpu.roll(wide, 1, 1, stride=1, stride_axis=0).astype(BF16)

    place = lax.broadcasted_iota(jnp.int32, (band, cin), 0)

    def shifted(x, by, edge):
        if by == 1:
            return jnp.where(place == 0, edge, pltpu.roll(x, 1, 0))
        return jnp.where(place == band - 1, edge, pltpu.roll(x, band - 1, 0))

    def lay(framed, i):
        if framed == 0:
            base = halo_row[0, i]
        elif framed == depth + 1:
            base = halo_row[1, i]
        else:
            base = images[i][framed - 1]
        tile = halo_col[i, framed].astype(F32)
        zero = jnp.zeros((1, cin), F32)
        enter_left = jnp.where(c == 0, zero, tile[TILE - 1 : TILE])
        enter_right = jnp.where(c == 0, tile[0:1], zero)
        wide = base.astype(F32)
        three = (
            shifted(wide, 1, enter_left).astype(BF16),
            base,
            shifted(wide, -1, enter_right).astype(BF16),
        )
        for row_tap in range(3):
            h = framed - row_tap
            if 0 <= h < depth:
                for k in range(3):
                    patch[i, h, :, pl.ds((row_tap * 3 + k) * cin, cin)] = three[k]

    inverse = 1.0 / math.sqrt(features)

    def ext_copy(h):
        return remote(
            right_ext.at[h, pl.ds(band, reach)], right_ext.at[h, pl.ds(0, reach)],
            ext_send.at[h], ext_recv.at[h], r, other,
        )

    def ret_copy(h):
        return remote(ret_out.at[h], ret_in.at[h], ret_send.at[h], ret_recv.at[h], r, other)

    def edge_copy(h, i):
        return remote(
            grad.at[i, h, pl.ds(near, TILE)], grad_edge.at[i, h], edge_send.at[i, h], edge_recv.at[i, h], r, other
        )

    def part_copy(side, i):
        target = r - 1 if side == 0 else r + 1
        return remote(
            part_out.at[side, i], part_in.at[1 - side, i], part_send.at[side, i], part_recv.at[1 - side, i],
            target, c,
        )

    @pl.when(c == 0)
    def _():
        right_ext[:, 0:reach] = jnp.zeros((depth, reach, features), BF16)

    def own_taps(h):
        return (0 if h > 0 else 1), (3 if h < depth - 1 else 2)

    def convolve(i, h, first, last):
        lanes = pl.ds(first * 3 * cin, (last - first) * 3 * cin)
        return matmul(patch[i, h, :, lanes], weight[lanes], ((1,), (0,)))

    def feature(i, h):
        first, last = own_taps(h)
        total = own_conv[i, h]
        if first > 0:
            total = total + convolve(i, h, 0, first)
        if last < 3:
            total = total + convolve(i, h, last, 3)
        return total.astype(BF16)

    def weight_term(i, h):
        return matmul(grad[i, h], patch[i, h], ((0,), (0,)))

    def spread_grad(i, h):
        zed[i, h, 0:band] = matmul(grad[i, h], weight[...], ((1,), (1,)))

    def spread_edge(i, h):
        edge_copy(h, i).wait_recv()
        zed[i, h, pl.ds(band, TILE)] = matmul(grad_edge[i, h], weight[...], ((1,), (1,)))

    def left_chain(h):
        right_ext[h, pl.ds(reach, band)] = feature(1, h)

        @pl.when(c == 0)
        def _():
            ext_copy(h).start()

        for s in range(blocks - 1, -1, -1):
            if s == 0:
                if h > 0:
                    early[...] += weight_term(1, h - 1)

                @pl.when(c == 1)
                def _():
                    ext_copy(h).wait_recv()

            window = right_ext[h, pl.ds(s * reach, 2 * reach)]
            out = matmul(band_m[h, s], window, ((1,), (0,)))
            grad[0, h, pl.ds(s * reach, reach)] = (out * inverse).astype(BF16)
        edge_copy(h, 0).start()
        spread_grad(0, h)

    def right_chain(h):
        left_feat[...] = feature(0, h)
        pending = None
        for s in range(blocks):
            both = matmul(band_m[h, s], left_feat[pl.ds(s * reach, reach)], ((0,), (0,)))
            head = both[:reach]
            if s == 0:
                ret_out[h] = head.astype(BF16)

                @pl.when(c == 1)
                def _():
                    ret_copy(h).start()
            else:
                grad[1, h, pl.ds((s - 1) * reach, reach)] = ((pending + head) * inverse).astype(BF16)
            pending = both[reach:]

        if h == 0:
            early[...] = weight_term(0, h)
        else:
            early[...] += weight_term(0, h)

        @pl.when(c == 0)
        def _():
            ret_copy(h).wait_recv()

        came = jnp.where(c == 0, ret_in[h].astype(F32), 0.0)
        grad[1, h, pl.ds(band - reach, reach)] = ((pending + came) * inverse).astype(BF16)
        edge_copy(h, 1).start()

    def gathered(i, goal):
        total = None
        for b in (0, 1, -1):
            inner = None
            enter = None
            for a in (-1, 0, 1):
                h = goal - a
                if not 0 <= h < depth:
                    continue
                lanes = pl.ds(((a + 1) * 3 + b + 1) * cin, cin)
                main = zed[i, h, 0:band, lanes]
                inner = main if inner is None else inner + main
                if b != 0:
                    line = zed[i, h, pl.ds(band, TILE), lanes]
                    enter = line if enter is None else enter + line
            if b == 0:
                total = inner
            elif b == 1:
                entering = jnp.where(c == 1, enter[TILE - 1 : TILE], 0.0)
                total = total + shifted(inner, 1, entering)
            else:
                entering = jnp.where(c == 0, enter[0:1], 0.0)
                total = total + shifted(inner, -1, entering)
        return total

    for load in loads[4:]:
        load.wait()
    for i in (1, 0):
        tile_mid(i).wait_recv()
        for framed in range(1, depth + 1):
            lay(framed, i)
    for i in (1, 0):
        for h in range(depth):
            own_conv[i, h] = convolve(i, h, *own_taps(h))

    @pl.when(has_down)
    def _():
        for i in (1, 0):
            tile_down(i).wait_send()
            down(i).wait_send()

    @pl.when(has_up)
    def _():
        for i in (1, 0):
            tile_up(i).start()
            up(i).start()

    hear_word(0)
    if rounds > 1:
        spread_word(1)

    def from_above(i):
        @pl.when(has_up)
        def _():
            tile_down(i).wait_recv()
            down(i).wait_recv()

        lay(0, i)

    def from_below(i):
        @pl.when(has_down)
        def _():
            tile_up(i).wait_recv()
            up(i).wait_recv()

        lay(depth + 1, i)

    def ready_part(side, goal, i):
        part_out[side, i] = gathered(i, goal).astype(BF16)

    def give(side, allowed, i):
        @pl.when(allowed)
        def _():
            part_copy(side, i).start()

    def entering(h, i):
        if h == 0:
            from_above(i)
        if h == depth - 1:
            from_below(i)

    def pair_copy(k):
        return remote(pair_out.at[k, other], pair_in.at[k], pair_send.at[k], pair_recv.at[k], r, other)

    scale = 1.0 / math.sqrt(2 * depth * band * group)
    for h in range(depth):
        entering(h, 1)
        left_chain(h)
        entering(h, 0)
        right_chain(h)
        if h == depth - 1:
            for k in range(3):
                lanes = pl.ds(k * 3 * cin, 3 * cin)
                total = matmul(grad[1, h], patch[1, h, :, lanes], ((0,), (0,)))
                total = (early[:, lanes] + total) * scale
                for s in range(rows):
                    for col in range(cols):
                        start = (s * cols + col) * quota
                        piece = total[start : start + quota]
                        acc[k, col, s % 2, s // 2] = piece
                        pair_out[k, col, s % 2, s // 2] = piece.astype(BF16)
                pair_copy(k).start()
        spread_grad(1, h)
        spread_edge(0, h)
        spread_edge(1, h)
        if h == 0:
            for i in (0, 1):
                ready_part(0, -1, i)
                give(0, has_up, i)
            if rounds > 1:
                hear_word(1)
            if rounds > 2:
                spread_word(2)
    for k in range(2, rounds):
        hear_word(k)
        if k + 1 < rounds:
            spread_word(k + 1)

    half = rows // 2
    place_in_half = r // 2
    parity = lax.rem(r, 2)
    across = r + 1 - 2 * parity

    def cross_copy(k):
        return remote(cross_out.at[k], cross_in.at[k], cross_send.at[k], cross_recv.at[k], across, c)

    def chunk_copy(k, i):
        goal = lax.rem(place_in_half + i, half)
        return remote(
            chunk.at[k, goal], landed.at[k, i], chunk_send.at[k, i], chunk_recv.at[k, i], 2 * goal + parity, c
        )

    for k in range(3):
        pair_copy(k).wait_recv()
        cross_out[k] = (acc[k, c, 1 - parity] + pair_in[k, 1 - parity].astype(F32)).astype(BF16)
        cross_copy(k).start()
        acc[k, c, parity] += pair_in[k, parity].astype(F32)


    outs = (gl_buf, gr_buf)

    def store(i, goal):
        return pltpu.make_async_copy(outs[i].at[goal], (gl_out, gr_out)[i].at[goal], store_sem.at[i, goal])

    def put(goal):
        for i in (0, 1):
            total = own_conv[i, goal, :, 0:cin]
            if goal == 0:
                total = total + jnp.where(has_up, part_in[0, i].astype(F32), 0.0)
            if goal == depth - 1:
                total = total + jnp.where(has_down, part_in[1, i].astype(F32), 0.0)
            outs[i][goal] = total.astype(BF16)
            store(i, goal).start()

    def last_copy(k):
        return remote(whole.at[k, c], whole.at[k, c], whole_send.at[k], whole_recv.at[k], r, other)

    for i in (0, 1):
        ready_part(1, depth, i)
        for goal in range(depth):
            own_conv[i, goal, :, 0:cin] = gathered(i, goal)

    for k in range(3):
        cross_copy(k).wait_recv()
        total = acc[k, c, parity] + cross_in[k].astype(F32)
        acc[k, c, parity] = total
        chunk[k] = total.astype(BF16)

        def start_chunk(i, carry):
            chunk_copy(k, i).start()
            return carry

        lax.fori_loop(1, half, start_chunk, 0)

    for i in (0, 1):
        give(1, has_down, i)

    @pl.when(has_down)
    def _():
        for i in (0, 1):
            part_copy(0, i).wait_recv()

    for goal in range(depth - 1, 0, -1):
        put(goal)

    for k in range(3):

        def wait_chunk(i, carry):
            chunk_copy(k, i).wait_recv()
            return carry

        def add_chunk(i, total):
            return total + landed[k, i].astype(F32)

        lax.fori_loop(1, half, wait_chunk, 0)
        whole[k, c] = lax.fori_loop(1, half, add_chunk, acc[k, c, parity, place_in_half])
        last_copy(k).start()

    @pl.when(has_up)
    def _():
        for i in (0, 1):
            part_copy(1, i).wait_recv()

    put(0)

    for k in range(3):
        last_copy(k).wait_recv()
        for col in range(cols):
            wg_buf[pl.ds(col * quota, quota), pl.ds(k * 3 * cin, 3 * cin)] = whole[k, col]

    whole_store = pltpu.make_async_copy(wg_buf, wg_out, load_sem.at[0])
    whole_store.start()
    for k in range(3):
        last_copy(k).wait_send()
        pair_copy(k).wait_send()
        cross_copy(k).wait_send()

        def drain(i, carry):
            chunk_copy(k, i).wait_send()
            return carry

        lax.fori_loop(1, half, drain, 0)
    for i in (0, 1):
        tile_mid(i).wait_send()
    for h in range(depth):
        for i in (0, 1):
            edge_copy(h, i).wait_send()

    @pl.when(has_down)
    def _():
        for i in (0, 1):
            part_copy(1, i).wait_send()

    @pl.when(has_up)
    def _():
        for i in (0, 1):
            tile_up(i).wait_send()
            up(i).wait_send()
            part_copy(0, i).wait_send()

    @pl.when(c == 0)
    def _():
        for h in range(depth):
            ext_copy(h).wait_send()

    @pl.when(c == 1)
    def _():
        for h in range(depth):
            ret_copy(h).wait_send()

    for i in (0, 1):
        for goal in range(depth):
            store(i, goal).wait()
    whole_store.wait()


def hand_over(a, b, w, a_out, b_out, w_out, a_mid, b_mid, w_mid, sem_in, sem_out):
    into = [
        pltpu.make_async_copy(src, mid, sem_in.at[k])
        for k, (src, mid) in enumerate(((a, a_mid), (b, b_mid), (w, w_mid)))
    ]
    out = [
        pltpu.make_async_copy(mid, dst, sem_out.at[k])
        for k, (mid, dst) in enumerate(((a_mid, a_out), (b_mid, b_out), (w_mid, w_out)))
    ]
    for copy in into:
        copy.start()
    for first, second in zip(into, out):
        first.wait()
        second.start()
    for copy in out:
        copy.wait()


def on_device(rows, cols, left, right, weight, l0, l1, l2, l3):
    depth, band, cin = left.shape
    taps, features = weight.shape
    reach = l0.shape[2]
    blocks = band // reach
    quota = features // (rows * cols)
    third = taps // 3
    l2 = jnp.swapaxes(l2, 1, 2)
    l3 = jnp.swapaxes(l3, 1, 2)
    dma = pltpu.SemaphoreType.DMA
    results = pl.pallas_call(
        functools.partial(kernel, rows, cols),
        out_shape=(
            jax.ShapeDtypeStruct(left.shape, BF16),
            jax.ShapeDtypeStruct(right.shape, BF16),
            jax.ShapeDtypeStruct((features // rows, taps), F32),
        ),
        in_specs=[pl.BlockSpec(memory_space=pl.ANY)] * 7,
        out_specs=(pl.BlockSpec(memory_space=pl.ANY),) * 3,
        scratch_shapes=[
            *(pltpu.VMEM(x.shape, BF16) for x in (left, right, left, right)),
            pltpu.VMEM((features // rows, taps), F32),
            *(pltpu.VMEM(x.shape, BF16) for x in (weight, l0, l1, l2, l3)),
            pltpu.VMEM((2, 2, band, cin), BF16),
            pltpu.VMEM((2, depth + 2, TILE, cin), BF16),
            pltpu.VMEM((depth, blocks, reach, 2 * reach), BF16),
            pltpu.VMEM((2, depth, band, taps), BF16),
            pltpu.VMEM((band, features), BF16),
            pltpu.VMEM((depth, reach + band, features), BF16),
            pltpu.VMEM((depth, reach, features), BF16),
            pltpu.VMEM((depth, reach, features), BF16),
            pltpu.VMEM((2, depth, band, features), BF16),
            pltpu.VMEM((2, depth, TILE, features), BF16),
            pltpu.VMEM((2, depth, band + TILE, taps), F32),
            pltpu.VMEM((2, 2, band, cin), BF16),
            pltpu.VMEM((2, 2, band, cin), BF16),
            pltpu.VMEM((2, depth, band, features), F32),
            pltpu.VMEM((3, cols, 2, rows // 2, quota, third), F32),
            pltpu.VMEM((features, taps), F32),
            pltpu.VMEM((3, cols, 2, rows // 2, quota, third), BF16),
            pltpu.VMEM((3, 2, rows // 2, quota, third), BF16),
            *(pltpu.VMEM((3, rows // 2, quota, third), BF16) for _ in range(4)),
            pltpu.VMEM((3, cols, quota, third), F32),
            dma((2, 2)), dma((2, 2)), dma((3, 2)), dma((3, 2)),
            dma((depth,)), dma((depth,)), dma((depth,)), dma((depth,)),
            dma((2, depth)), dma((2, depth)), dma((2, 2)), dma((2, 2)),
            dma((3,)), dma((3,)), dma((3,)), dma((3,)), dma((3, rows // 2)), dma((3, rows // 2)), dma((3,)), dma((3,)), dma((7,)),
            dma((2, depth)), pltpu.SemaphoreType.REGULAR(((rows - 1).bit_length(), 2)),
        ],
        compiler_params=pltpu.CompilerParams(
            collective_id=0, has_side_effects=True, vmem_limit_bytes=60 * 1024 * 1024
        ),
        name="stereo_backward",
    )(left, right, weight, l0, l1, l2, l3)
    hbm = pl.BlockSpec(memory_space=pl.ANY)
    shapes = tuple(jax.ShapeDtypeStruct(x.shape, x.dtype) for x in results)
    return pl.pallas_call(
        hand_over,
        out_shape=shapes,
        in_specs=[hbm] * 3,
        out_specs=(hbm,) * 3,
        scratch_shapes=[*(pltpu.VMEM(x.shape, x.dtype) for x in results), dma((3,)), dma((3,))],
        name="hand_over",
    )(*results)


def solution(mesh):
    banded = P(("pairs", "rows"), "cols", None)
    return jax.shard_map(
        functools.partial(on_device, mesh.shape["rows"], mesh.shape["cols"]),
        mesh=mesh,
        in_specs=(banded, banded, P(), banded, banded, banded, banded),
        out_specs=(banded, banded, P(("pairs", "rows"), None)),
        check_vma=False,
    )
```

```python
import functools
import math

import jax
import jax.numpy as jnp
from jax import lax
from jax.experimental import pallas as pl
from jax.experimental.pallas import tpu as pltpu
from jax.sharding import PartitionSpec as P

F32 = jnp.float32
BF16 = jnp.bfloat16
TILE = 16


def remote(src, dst, send, recv, row, col):
    return pltpu.make_async_remote_copy(
        src_ref=src,
        dst_ref=dst,
        send_sem=send,
        recv_sem=recv,
        device_id={"rows": row, "cols": col},
        device_id_type=pl.DeviceIdType.MESH,
    )


def matmul(a, b, dims):
    return lax.dot_general(a, b, (dims, ((), ())), preferred_element_type=F32)


def expansion(levels, reach, factor):
    source = lax.broadcasted_iota(jnp.int32, (levels, reach), 0)
    target = (reach - 1) - lax.broadcasted_iota(jnp.int32, (levels, reach), 1)
    bits = factor.bit_length() - 1
    hit = lax.shift_right_logical(target, jnp.int32(bits)) == source
    return jnp.where(hit, 1.0 / factor, 0.0).astype(BF16)


def kernel(
    rows, cols, left_hbm, right_hbm, weight_hbm, l0_hbm, l1_hbm, l2_hbm, l3_hbm, gl_out, gr_out, wg_out,
    left, right, gl_buf, gr_buf, wg_buf, weight, l0, l1, l2, l3, halo_row, halo_col, band_m, patch, left_feat, right_ext, ret_out, ret_in,
    grad, grad_edge, zed, part_out, part_in, own_conv, acc, early, pair_out, pair_in, cross_out, cross_in, chunk, landed, whole,
    row_send, row_recv, col_send, col_recv, ext_send, ext_recv, ret_send, ret_recv,
    edge_send, edge_recv, part_send, part_recv, pair_send, pair_recv, cross_send, cross_recv, chunk_send, chunk_recv, whole_send, whole_recv, load_sem, store_sem, known,
):
    depth, band, cin = left.shape
    features = weight.shape[1]
    reach = l0.shape[2]
    blocks = band // reach
    quota = features // (rows * cols)
    r = lax.axis_index("rows")
    c = lax.axis_index("cols")
    other = 1 - c
    images = (left, right)
    sources = (left_hbm, right_hbm)
    group = rows * cols
    has_up = r > 0
    has_down = r < rows - 1

    barrier = pltpu.get_barrier_semaphore()

    def tell(semaphore, row, col):
        pl.semaphore_signal(
            semaphore, inc=1, device_id={"rows": row, "cols": col}, device_id_type=pl.DeviceIdType.MESH
        )

    tell(barrier, r, other)

    @pl.when(has_up)
    def _():
        for col in (c, other):
            tell(barrier, r - 1, col)

    @pl.when(has_down)
    def _():
        for col in (c, other):
            tell(barrier, r + 1, col)

    loads = [
        pltpu.make_async_copy(src, dst, load_sem.at[k])
        for k, (src, dst) in enumerate(
            (
                (l0_hbm, l0), (l1_hbm, l1), (l2_hbm, l2), (l3_hbm, l3),
                (right_hbm, right), (left_hbm, left), (weight_hbm, weight),
            )
        )
    ]
    for load in loads:
        load.start()
    pl.semaphore_wait(barrier, 1 + 2 * has_up.astype(jnp.int32) + 2 * has_down.astype(jnp.int32))

    rounds = (rows - 1).bit_length()

    def spread_word(k):
        @pl.when(r >= 2**k)
        def _():
            tell(known.at[k, 1], r - 2**k, c)

        @pl.when(r + 2**k < rows)
        def _():
            tell(known.at[k, 0], r + 2**k, c)

    def hear_word(k):
        @pl.when(r >= 2**k)
        def _():
            pl.semaphore_wait(known.at[k, 0], 1)

        @pl.when(r + 2**k < rows)
        def _():
            pl.semaphore_wait(known.at[k, 1], 1)

    near = pl.multiple_of(other * (band - TILE), TILE)

    def down(i):
        return remote(sources[i].at[depth - 1], halo_row.at[0, i], row_send.at[0, i], row_recv.at[0, i], r + 1, c)

    def up(i):
        return remote(sources[i].at[0], halo_row.at[1, i], row_send.at[1, i], row_recv.at[1, i], r - 1, c)

    def tile_mid(i):
        return remote(
            sources[i].at[:, pl.ds(near, TILE)], halo_col.at[i, pl.ds(1, depth)],
            col_send.at[0, i], col_recv.at[0, i], r, other,
        )

    def tile_down(i):
        return remote(
            sources[i].at[depth - 1, pl.ds(near, TILE)], halo_col.at[i, 0],
            col_send.at[1, i], col_recv.at[1, i], r + 1, other,
        )

    def tile_up(i):
        return remote(
            sources[i].at[0, pl.ds(near, TILE)], halo_col.at[i, depth + 1],
            col_send.at[2, i], col_recv.at[2, i], r - 1, other,
        )

    for i in (1, 0):
        tile_mid(i).start()

    @pl.when(has_down)
    def _():
        for i in (1, 0):
            tile_down(i).start()
            down(i).start()

    spread_word(0)

    @pl.when(r == 0)
    def _():
        halo_row[0] = jnp.zeros_like(halo_row[0])
        for i in (0, 1):
            halo_col[i, 0] = jnp.zeros_like(halo_col[i, 0])

    @pl.when(r == rows - 1)
    def _():
        halo_row[1] = jnp.zeros_like(halo_row[1])
        for i in (0, 1):
            halo_col[i, depth + 1] = jnp.zeros_like(halo_col[i, depth + 1])

    spread = [expansion(count, reach, reach // count) for count in (reach, l1.shape[2], l2.shape[1], l3.shape[1])]
    for load in loads[:4]:
        load.wait()
    for h in range(depth):
        for s in range(blocks):
            at = pl.ds(s * reach, reach)
            total = matmul(l0[h, at], spread[0], ((1,), (0,)))
            total = total + matmul(l1[h, at], spread[1], ((1,), (0,)))
            for level, way in zip((l2, l3), spread[2:]):
                total = total + matmul(level[h, :, at], way, ((0,), (0,)))
            total = total.astype(BF16).astype(F32)
            wide = jnp.concatenate([total, jnp.zeros_like(total)], axis=1)
            band_m[h, s] = pltpu.roll(wide, 1, 1, stride=1, stride_axis=0).astype(BF16)

    place = lax.broadcasted_iota(jnp.int32, (band, cin), 0)

    def shifted(x, by, edge):
        if by == 1:
            return jnp.where(place == 0, edge, pltpu.roll(x, 1, 0))
        return jnp.where(place == band - 1, edge, pltpu.roll(x, band - 1, 0))

    def lay(framed, i):
        if framed == 0:
            base = halo_row[0, i]
        elif framed == depth + 1:
            base = halo_row[1, i]
        else:
            base = images[i][framed - 1]
        tile = halo_col[i, framed].astype(F32)
        zero = jnp.zeros((1, cin), F32)
        enter_left = jnp.where(c == 0, zero, tile[TILE - 1 : TILE])
        enter_right = jnp.where(c == 0, tile[0:1], zero)
        wide = base.astype(F32)
        three = (
            shifted(wide, 1, enter_left).astype(BF16),
            base,
            shifted(wide, -1, enter_right).astype(BF16),
        )
        for row_tap in range(3):
            h = framed - row_tap
            if 0 <= h < depth:
                for k in range(3):
                    patch[i, h, :, pl.ds((row_tap * 3 + k) * cin, cin)] = three[k]

    inverse = 1.0 / math.sqrt(features)

    def ext_copy(h):
        return remote(
            right_ext.at[h, pl.ds(band, reach)], right_ext.at[h, pl.ds(0, reach)],
            ext_send.at[h], ext_recv.at[h], r, other,
        )

    def ret_copy(h):
        return remote(ret_out.at[h], ret_in.at[h], ret_send.at[h], ret_recv.at[h], r, other)

    def edge_copy(h, i):
        return remote(
            grad.at[i, h, pl.ds(near, TILE)], grad_edge.at[i, h], edge_send.at[i, h], edge_recv.at[i, h], r, other
        )

    def part_copy(side, i):
        target = r - 1 if side == 0 else r + 1
        return remote(
            part_out.at[side, i], part_in.at[1 - side, i], part_send.at[side, i], part_recv.at[1 - side, i],
            target, c,
        )

    @pl.when(c == 0)
    def _():
        right_ext[:, 0:reach] = jnp.zeros((depth, reach, features), BF16)

    def own_taps(h):
        return (0 if h > 0 else 1), (3 if h < depth - 1 else 2)

    def convolve(i, h, first, last):
        lanes = pl.ds(first * 3 * cin, (last - first) * 3 * cin)
        return matmul(patch[i, h, :, lanes], weight[lanes], ((1,), (0,)))

    def feature(i, h):
        first, last = own_taps(h)
        total = own_conv[i, h]
        if first > 0:
            total = total + convolve(i, h, 0, first)
        if last < 3:
            total = total + convolve(i, h, last, 3)
        return total.astype(BF16)

    def weight_term(i, h):
        return matmul(grad[i, h], patch[i, h], ((0,), (0,)))

    def spread_grad(i, h):
        zed[i, h, 0:band] = matmul(grad[i, h], weight[...], ((1,), (1,)))

    def spread_edge(i, h):
        edge_copy(h, i).wait_recv()
        zed[i, h, pl.ds(band, TILE)] = matmul(grad_edge[i, h], weight[...], ((1,), (1,)))

    def left_chain(h):
        right_ext[h, pl.ds(reach, band)] = feature(1, h)

        @pl.when(c == 0)
        def _():
            ext_copy(h).start()

        for s in range(blocks - 1, -1, -1):
            if s == 0:
                if h > 0:
                    early[...] += weight_term(1, h - 1)

                @pl.when(c == 1)
                def _():
                    ext_copy(h).wait_recv()

            window = right_ext[h, pl.ds(s * reach, 2 * reach)]
            out = matmul(band_m[h, s], window, ((1,), (0,)))
            grad[0, h, pl.ds(s * reach, reach)] = (out * inverse).astype(BF16)
        edge_copy(h, 0).start()
        spread_grad(0, h)

    def right_chain(h):
        left_feat[...] = feature(0, h)
        pending = None
        for s in range(blocks):
            both = matmul(band_m[h, s], left_feat[pl.ds(s * reach, reach)], ((0,), (0,)))
            head = both[:reach]
            if s == 0:
                ret_out[h] = head.astype(BF16)

                @pl.when(c == 1)
                def _():
                    ret_copy(h).start()
            else:
                grad[1, h, pl.ds((s - 1) * reach, reach)] = ((pending + head) * inverse).astype(BF16)
            pending = both[reach:]

        if h == 0:
            early[...] = weight_term(0, h)
        else:
            early[...] += weight_term(0, h)

        @pl.when(c == 0)
        def _():
            ret_copy(h).wait_recv()

        came = jnp.where(c == 0, ret_in[h].astype(F32), 0.0)
        grad[1, h, pl.ds(band - reach, reach)] = ((pending + came) * inverse).astype(BF16)
        edge_copy(h, 1).start()

    def gathered(i, goal):
        total = None
        for b in (0, 1, -1):
            inner = None
            enter = None
            for a in (-1, 0, 1):
                h = goal - a
                if not 0 <= h < depth:
                    continue
                lanes = pl.ds(((a + 1) * 3 + b + 1) * cin, cin)
                main = zed[i, h, 0:band, lanes]
                inner = main if inner is None else inner + main
                if b != 0:
                    line = zed[i, h, pl.ds(band, TILE), lanes]
                    enter = line if enter is None else enter + line
            if b == 0:
                total = inner
            elif b == 1:
                entering = jnp.where(c == 1, enter[TILE - 1 : TILE], 0.0)
                total = total + shifted(inner, 1, entering)
            else:
                entering = jnp.where(c == 0, enter[0:1], 0.0)
                total = total + shifted(inner, -1, entering)
        return total

    for load in loads[4:]:
        load.wait()
    for i in (1, 0):
        tile_mid(i).wait_recv()
        for framed in range(1, depth + 1):
            lay(framed, i)
    for i in (1, 0):
        for h in range(depth):
            own_conv[i, h] = convolve(i, h, *own_taps(h))

    @pl.when(has_down)
    def _():
        for i in (1, 0):
            tile_down(i).wait_send()
            down(i).wait_send()

    @pl.when(has_up)
    def _():
        for i in (1, 0):
            tile_up(i).start()
            up(i).start()

    hear_word(0)
    if rounds > 1:
        spread_word(1)

    def from_above(i):
        @pl.when(has_up)
        def _():
            tile_down(i).wait_recv()
            down(i).wait_recv()

        lay(0, i)

    def from_below(i):
        @pl.when(has_down)
        def _():
            tile_up(i).wait_recv()
            up(i).wait_recv()

        lay(depth + 1, i)

    def ready_part(side, goal, i):
        part_out[side, i] = gathered(i, goal).astype(BF16)

    def give(side, allowed, i):
        @pl.when(allowed)
        def _():
            part_copy(side, i).start()

    def entering(h, i):
        if h == 0:
            from_above(i)
        if h == depth - 1:
            from_below(i)

    def pair_copy(k):
        return remote(pair_out.at[k, other], pair_in.at[k], pair_send.at[k], pair_recv.at[k], r, other)

    scale = 1.0 / math.sqrt(2 * depth * band * group)
    for h in range(depth):
        entering(h, 1)
        left_chain(h)
        if h == 0:
            spread_edge(0, 0)
            ready_part(0, -1, 0)
            give(0, has_up, 0)
        entering(h, 0)
        right_chain(h)
        if h == depth - 1:
            for k in range(3):
                lanes = pl.ds(k * 3 * cin, 3 * cin)
                total = matmul(grad[1, h], patch[1, h, :, lanes], ((0,), (0,)))
                total = (early[:, lanes] + total) * scale
                for s in range(rows):
                    for col in range(cols):
                        start = (s * cols + col) * quota
                        piece = total[start : start + quota]
                        acc[k, col, s % 2, s // 2] = piece
                        pair_out[k, col, s % 2, s // 2] = piece.astype(BF16)
                pair_copy(k).start()
        spread_grad(1, h)
        if h > 0:
            spread_edge(0, h)
        spread_edge(1, h)
        if h == 0:
            ready_part(0, -1, 1)
            give(0, has_up, 1)
            if rounds > 1:
                hear_word(1)
            if rounds > 2:
                spread_word(2)
    for k in range(2, rounds):
        hear_word(k)
        if k + 1 < rounds:
            spread_word(k + 1)

    half = rows // 2
    place_in_half = r // 2
    parity = lax.rem(r, 2)
    across = r + 1 - 2 * parity

    def cross_copy(k):
        return remote(cross_out.at[k], cross_in.at[k], cross_send.at[k], cross_recv.at[k], across, c)

    def chunk_copy(k, i):
        goal = lax.rem(place_in_half + i, half)
        return remote(
            chunk.at[k, goal], landed.at[k, i], chunk_send.at[k, i], chunk_recv.at[k, i], 2 * goal + parity, c
        )

    for k in range(3):
        pair_copy(k).wait_recv()
        cross_out[k] = (acc[k, c, 1 - parity] + pair_in[k, 1 - parity].astype(F32)).astype(BF16)
        cross_copy(k).start()
        acc[k, c, parity] += pair_in[k, parity].astype(F32)


    outs = (gl_buf, gr_buf)

    def store(i, goal):
        return pltpu.make_async_copy(outs[i].at[goal], (gl_out, gr_out)[i].at[goal], store_sem.at[i, goal])

    def put(goal):
        for i in (0, 1):
            total = own_conv[i, goal, :, 0:cin]
            if goal == 0:
                total = total + jnp.where(has_up, part_in[0, i].astype(F32), 0.0)
            if goal == depth - 1:
                total = total + jnp.where(has_down, part_in[1, i].astype(F32), 0.0)
            outs[i][goal] = total.astype(BF16)
            store(i, goal).start()

    def last_copy(k):
        return remote(whole.at[k, c], whole.at[k, c], whole_send.at[k], whole_recv.at[k], r, other)

    for i in (0, 1):
        ready_part(1, depth, i)
        for goal in range(depth):
            own_conv[i, goal, :, 0:cin] = gathered(i, goal)

    for k in range(3):
        cross_copy(k).wait_recv()
        total = acc[k, c, parity] + cross_in[k].astype(F32)
        acc[k, c, parity] = total
        chunk[k] = total.astype(BF16)

        def start_chunk(i, carry):
            chunk_copy(k, i).start()
            return carry

        lax.fori_loop(1, half, start_chunk, 0)
        if k == 1:
            give(1, has_down, 0)
            give(1, has_down, 1)


    @pl.when(has_down)
    def _():
        for i in (0, 1):
            part_copy(0, i).wait_recv()

    for goal in range(depth - 1, 0, -1):
        put(goal)

    for k in range(3):

        def wait_chunk(i, carry):
            chunk_copy(k, i).wait_recv()
            return carry

        def add_chunk(i, total):
            return total + landed[k, i].astype(F32)

        lax.fori_loop(1, half, wait_chunk, 0)
        whole[k, c] = lax.fori_loop(1, half, add_chunk, acc[k, c, parity, place_in_half])
        last_copy(k).start()

    @pl.when(has_up)
    def _():
        for i in (0, 1):
            part_copy(1, i).wait_recv()

    put(0)

    for k in range(3):
        last_copy(k).wait_recv()
        for col in range(cols):
            wg_buf[pl.ds(col * quota, quota), pl.ds(k * 3 * cin, 3 * cin)] = whole[k, col]

    whole_store = pltpu.make_async_copy(wg_buf, wg_out, load_sem.at[0])
    whole_store.start()
    for k in range(3):
        last_copy(k).wait_send()
        pair_copy(k).wait_send()
        cross_copy(k).wait_send()

        def drain(i, carry):
            chunk_copy(k, i).wait_send()
            return carry

        lax.fori_loop(1, half, drain, 0)
    for i in (0, 1):
        tile_mid(i).wait_send()
    for h in range(depth):
        for i in (0, 1):
            edge_copy(h, i).wait_send()

    @pl.when(has_down)
    def _():
        for i in (0, 1):
            part_copy(1, i).wait_send()

    @pl.when(has_up)
    def _():
        for i in (0, 1):
            tile_up(i).wait_send()
            up(i).wait_send()
            part_copy(0, i).wait_send()

    @pl.when(c == 0)
    def _():
        for h in range(depth):
            ext_copy(h).wait_send()

    @pl.when(c == 1)
    def _():
        for h in range(depth):
            ret_copy(h).wait_send()

    for i in (0, 1):
        for goal in range(depth):
            store(i, goal).wait()
    whole_store.wait()


def hand_over(a, b, w, a_out, b_out, w_out, a_mid, b_mid, w_mid, sem_in, sem_out):
    into = [
        pltpu.make_async_copy(src, mid, sem_in.at[k])
        for k, (src, mid) in enumerate(((a, a_mid), (b, b_mid), (w, w_mid)))
    ]
    out = [
        pltpu.make_async_copy(mid, dst, sem_out.at[k])
        for k, (mid, dst) in enumerate(((a_mid, a_out), (b_mid, b_out), (w_mid, w_out)))
    ]
    for copy in into:
        copy.start()
    for first, second in zip(into, out):
        first.wait()
        second.start()
    for copy in out:
        copy.wait()


def on_device(rows, cols, left, right, weight, l0, l1, l2, l3):
    depth, band, cin = left.shape
    taps, features = weight.shape
    reach = l0.shape[2]
    blocks = band // reach
    quota = features // (rows * cols)
    third = taps // 3
    l2 = jnp.swapaxes(l2, 1, 2)
    l3 = jnp.swapaxes(l3, 1, 2)
    dma = pltpu.SemaphoreType.DMA
    results = pl.pallas_call(
        functools.partial(kernel, rows, cols),
        out_shape=(
            jax.ShapeDtypeStruct(left.shape, BF16),
            jax.ShapeDtypeStruct(right.shape, BF16),
            jax.ShapeDtypeStruct((features // rows, taps), F32),
        ),
        in_specs=[pl.BlockSpec(memory_space=pl.ANY)] * 7,
        out_specs=(pl.BlockSpec(memory_space=pl.ANY),) * 3,
        scratch_shapes=[
            *(pltpu.VMEM(x.shape, BF16) for x in (left, right, left, right)),
            pltpu.VMEM((features // rows, taps), F32),
            *(pltpu.VMEM(x.shape, BF16) for x in (weight, l0, l1, l2, l3)),
            pltpu.VMEM((2, 2, band, cin), BF16),
            pltpu.VMEM((2, depth + 2, TILE, cin), BF16),
            pltpu.VMEM((depth, blocks, reach, 2 * reach), BF16),
            pltpu.VMEM((2, depth, band, taps), BF16),
            pltpu.VMEM((band, features), BF16),
            pltpu.VMEM((depth, reach + band, features), BF16),
            pltpu.VMEM((depth, reach, features), BF16),
            pltpu.VMEM((depth, reach, features), BF16),
            pltpu.VMEM((2, depth, band, features), BF16),
            pltpu.VMEM((2, depth, TILE, features), BF16),
            pltpu.VMEM((2, depth, band + TILE, taps), F32),
            pltpu.VMEM((2, 2, band, cin), BF16),
            pltpu.VMEM((2, 2, band, cin), BF16),
            pltpu.VMEM((2, depth, band, features), F32),
            pltpu.VMEM((3, cols, 2, rows // 2, quota, third), F32),
            pltpu.VMEM((features, taps), F32),
            pltpu.VMEM((3, cols, 2, rows // 2, quota, third), BF16),
            pltpu.VMEM((3, 2, rows // 2, quota, third), BF16),
            *(pltpu.VMEM((3, rows // 2, quota, third), BF16) for _ in range(4)),
            pltpu.VMEM((3, cols, quota, third), F32),
            dma((2, 2)), dma((2, 2)), dma((3, 2)), dma((3, 2)),
            dma((depth,)), dma((depth,)), dma((depth,)), dma((depth,)),
            dma((2, depth)), dma((2, depth)), dma((2, 2)), dma((2, 2)),
            dma((3,)), dma((3,)), dma((3,)), dma((3,)), dma((3, rows // 2)), dma((3, rows // 2)), dma((3,)), dma((3,)), dma((7,)),
            dma((2, depth)), pltpu.SemaphoreType.REGULAR(((rows - 1).bit_length(), 2)),
        ],
        compiler_params=pltpu.CompilerParams(
            collective_id=0, has_side_effects=True, vmem_limit_bytes=60 * 1024 * 1024
        ),
        name="stereo_backward",
    )(left, right, weight, l0, l1, l2, l3)
    hbm = pl.BlockSpec(memory_space=pl.ANY)
    shapes = tuple(jax.ShapeDtypeStruct(x.shape, x.dtype) for x in results)
    return pl.pallas_call(
        hand_over,
        out_shape=shapes,
        in_specs=[hbm] * 3,
        out_specs=(hbm,) * 3,
        scratch_shapes=[*(pltpu.VMEM(x.shape, x.dtype) for x in results), dma((3,)), dma((3,))],
        name="hand_over",
    )(*results)


def solution(mesh):
    banded = P(("pairs", "rows"), "cols", None)
    return jax.shard_map(
        functools.partial(on_device, mesh.shape["rows"], mesh.shape["cols"]),
        mesh=mesh,
        in_specs=(banded, banded, P(), banded, banded, banded, banded),
        out_specs=(banded, banded, P(("pairs", "rows"), None)),
        check_vma=False,
    )
```

```python
import functools
import math

import jax
import jax.numpy as jnp
from jax import lax
from jax.experimental import pallas as pl
from jax.experimental.pallas import tpu as pltpu
from jax.sharding import PartitionSpec as P

F32 = jnp.float32
BF16 = jnp.bfloat16
TILE = 16


def remote(src, dst, send, recv, row, col):
    return pltpu.make_async_remote_copy(
        src_ref=src,
        dst_ref=dst,
        send_sem=send,
        recv_sem=recv,
        device_id={"rows": row, "cols": col},
        device_id_type=pl.DeviceIdType.MESH,
    )


def matmul(a, b, dims):
    return lax.dot_general(a, b, (dims, ((), ())), preferred_element_type=F32)


def expansion(levels, reach, factor):
    source = lax.broadcasted_iota(jnp.int32, (levels, reach), 0)
    target = (reach - 1) - lax.broadcasted_iota(jnp.int32, (levels, reach), 1)
    bits = factor.bit_length() - 1
    hit = lax.shift_right_logical(target, jnp.int32(bits)) == source
    return jnp.where(hit, 1.0 / factor, 0.0).astype(BF16)


def kernel(
    rows, cols, left_hbm, right_hbm, weight_hbm, l0_hbm, l1_hbm, l2_hbm, l3_hbm, gl_out, gr_out, wg_out,
    left, right, gl_buf, gr_buf, wg_buf, weight, l0, l1, l2, l3, halo_row, halo_col, band_m, patch, left_feat, right_ext, ret_out, ret_in,
    grad, grad_edge, zed, part_out, part_in, own_conv, acc, early, pair_out, pair_in, cross_out, cross_in, chunk, landed, whole,
    row_send, row_recv, col_send, col_recv, ext_send, ext_recv, ret_send, ret_recv,
    edge_send, edge_recv, part_send, part_recv, pair_send, pair_recv, cross_send, cross_recv, chunk_send, chunk_recv, whole_send, whole_recv, load_sem, store_sem, known,
):
    depth, band, cin = left.shape
    features = weight.shape[1]
    reach = l0.shape[2]
    blocks = band // reach
    quota = features // (rows * cols)
    r = lax.axis_index("rows")
    c = lax.axis_index("cols")
    other = 1 - c
    images = (left, right)
    sources = (left_hbm, right_hbm)
    group = rows * cols
    has_up = r > 0
    has_down = r < rows - 1

    barrier = pltpu.get_barrier_semaphore()

    def tell(semaphore, row, col):
        pl.semaphore_signal(
            semaphore, inc=1, device_id={"rows": row, "cols": col}, device_id_type=pl.DeviceIdType.MESH
        )

    tell(barrier, r, other)

    @pl.when(has_up)
    def _():
        for col in (c, other):
            tell(barrier, r - 1, col)

    @pl.when(has_down)
    def _():
        for col in (c, other):
            tell(barrier, r + 1, col)

    loads = [
        pltpu.make_async_copy(src, dst, load_sem.at[k])
        for k, (src, dst) in enumerate(
            (
                (l0_hbm, l0), (l1_hbm, l1), (l2_hbm, l2), (l3_hbm, l3),
                (right_hbm, right), (left_hbm, left), (weight_hbm, weight),
            )
        )
    ]
    for load in loads:
        load.start()
    pl.semaphore_wait(barrier, 1 + 2 * has_up.astype(jnp.int32) + 2 * has_down.astype(jnp.int32))

    rounds = (rows - 1).bit_length()

    def spread_word(k):
        @pl.when(r >= 2**k)
        def _():
            tell(known.at[k, 1], r - 2**k, c)

        @pl.when(r + 2**k < rows)
        def _():
            tell(known.at[k, 0], r + 2**k, c)

    def hear_word(k):
        @pl.when(r >= 2**k)
        def _():
            pl.semaphore_wait(known.at[k, 0], 1)

        @pl.when(r + 2**k < rows)
        def _():
            pl.semaphore_wait(known.at[k, 1], 1)

    near = pl.multiple_of(other * (band - TILE), TILE)

    def down(i):
        return remote(sources[i].at[depth - 1], halo_row.at[0, i], row_send.at[0, i], row_recv.at[0, i], r + 1, c)

    def up(i):
        return remote(sources[i].at[0], halo_row.at[1, i], row_send.at[1, i], row_recv.at[1, i], r - 1, c)

    def tile_mid(i):
        return remote(
            sources[i].at[:, pl.ds(near, TILE)], halo_col.at[i, pl.ds(1, depth)],
            col_send.at[0, i], col_recv.at[0, i], r, other,
        )

    def tile_down(i):
        return remote(
            sources[i].at[depth - 1, pl.ds(near, TILE)], halo_col.at[i, 0],
            col_send.at[1, i], col_recv.at[1, i], r + 1, other,
        )

    def tile_up(i):
        return remote(
            sources[i].at[0, pl.ds(near, TILE)], halo_col.at[i, depth + 1],
            col_send.at[2, i], col_recv.at[2, i], r - 1, other,
        )

    for i in (1, 0):
        tile_mid(i).start()

    @pl.when(has_down)
    def _():
        for i in (1, 0):
            tile_down(i).start()
            down(i).start()

    spread_word(0)

    @pl.when(r == 0)
    def _():
        halo_row[0] = jnp.zeros_like(halo_row[0])
        for i in (0, 1):
            halo_col[i, 0] = jnp.zeros_like(halo_col[i, 0])

    @pl.when(r == rows - 1)
    def _():
        halo_row[1] = jnp.zeros_like(halo_row[1])
        for i in (0, 1):
            halo_col[i, depth + 1] = jnp.zeros_like(halo_col[i, depth + 1])

    spread = [expansion(count, reach, reach // count) for count in (reach, l1.shape[2], l2.shape[1], l3.shape[1])]
    for load in loads[:4]:
        load.wait()
    for h in range(depth):
        for s in range(blocks):
            at = pl.ds(s * reach, reach)
            total = matmul(l0[h, at], spread[0], ((1,), (0,)))
            total = total + matmul(l1[h, at], spread[1], ((1,), (0,)))
            for level, way in zip((l2, l3), spread[2:]):
                total = total + matmul(level[h, :, at], way, ((0,), (0,)))
            total = total.astype(BF16).astype(F32)
            wide = jnp.concatenate([total, jnp.zeros_like(total)], axis=1)
            band_m[h, s] = pltpu.roll(wide, 1, 1, stride=1, stride_axis=0).astype(BF16)

    place = lax.broadcasted_iota(jnp.int32, (band, cin), 0)

    def shifted(x, by, edge):
        if by == 1:
            return jnp.where(place == 0, edge, pltpu.roll(x, 1, 0))
        return jnp.where(place == band - 1, edge, pltpu.roll(x, band - 1, 0))

    def lay(framed, i):
        if framed == 0:
            base = halo_row[0, i]
        elif framed == depth + 1:
            base = halo_row[1, i]
        else:
            base = images[i][framed - 1]
        tile = halo_col[i, framed].astype(F32)
        zero = jnp.zeros((1, cin), F32)
        enter_left = jnp.where(c == 0, zero, tile[TILE - 1 : TILE])
        enter_right = jnp.where(c == 0, tile[0:1], zero)
        wide = base.astype(F32)
        three = (
            shifted(wide, 1, enter_left).astype(BF16),
            base,
            shifted(wide, -1, enter_right).astype(BF16),
        )
        for row_tap in range(3):
            h = framed - row_tap
            if 0 <= h < depth:
                for k in range(3):
                    patch[i, h, :, pl.ds((row_tap * 3 + k) * cin, cin)] = three[k]

    inverse = 1.0 / math.sqrt(features)

    def ext_copy(h):
        return remote(
            right_ext.at[h, pl.ds(band, reach)], right_ext.at[h, pl.ds(0, reach)],
            ext_send.at[h], ext_recv.at[h], r, other,
        )

    def ret_copy(h):
        return remote(ret_out.at[h], ret_in.at[h], ret_send.at[h], ret_recv.at[h], r, other)

    def edge_copy(h, i):
        return remote(
            grad.at[i, h, pl.ds(near, TILE)], grad_edge.at[i, h], edge_send.at[i, h], edge_recv.at[i, h], r, other
        )

    def part_copy(side, i):
        target = r - 1 if side == 0 else r + 1
        return remote(
            part_out.at[side, i], part_in.at[1 - side, i], part_send.at[side, i], part_recv.at[1 - side, i],
            target, c,
        )

    @pl.when(c == 0)
    def _():
        right_ext[:, 0:reach] = jnp.zeros((depth, reach, features), BF16)

    def own_taps(h):
        return (0 if h > 0 else 1), (3 if h < depth - 1 else 2)

    def convolve(i, h, first, last):
        lanes = pl.ds(first * 3 * cin, (last - first) * 3 * cin)
        return matmul(patch[i, h, :, lanes], weight[lanes], ((1,), (0,)))

    def feature(i, h):
        first, last = own_taps(h)
        total = own_conv[i, h]
        if first > 0:
            total = total + convolve(i, h, 0, first)
        if last < 3:
            total = total + convolve(i, h, last, 3)
        return total.astype(BF16)

    def weight_term(i, h):
        return matmul(grad[i, h], patch[i, h], ((0,), (0,)))

    def spread_grad(i, h):
        zed[i, h, 0:band] = matmul(grad[i, h], weight[...], ((1,), (1,)))

    def spread_edge(i, h):
        edge_copy(h, i).wait_recv()
        zed[i, h, pl.ds(band, TILE)] = matmul(grad_edge[i, h], weight[...], ((1,), (1,)))

    def left_chain(h):
        right_ext[h, pl.ds(reach, band)] = feature(1, h)

        @pl.when(c == 0)
        def _():
            ext_copy(h).start()

        for s in range(blocks - 1, -1, -1):
            if s == 0:
                if h > 0:
                    early[...] += weight_term(1, h - 1)

                @pl.when(c == 1)
                def _():
                    ext_copy(h).wait_recv()

            window = right_ext[h, pl.ds(s * reach, 2 * reach)]
            out = matmul(band_m[h, s], window, ((1,), (0,)))
            grad[0, h, pl.ds(s * reach, reach)] = (out * inverse).astype(BF16)
        edge_copy(h, 0).start()
        spread_grad(0, h)

    def right_chain(h):
        left_feat[...] = feature(0, h)
        pending = None
        for s in range(blocks):
            both = matmul(band_m[h, s], left_feat[pl.ds(s * reach, reach)], ((0,), (0,)))
            head = both[:reach]
            if s == 0:
                ret_out[h] = head.astype(BF16)

                @pl.when(c == 1)
                def _():
                    ret_copy(h).start()
            else:
                grad[1, h, pl.ds((s - 1) * reach, reach)] = ((pending + head) * inverse).astype(BF16)
            pending = both[reach:]

        if h == 0:
            early[...] = weight_term(0, h)
        else:
            early[...] += weight_term(0, h)

        @pl.when(c == 0)
        def _():
            ret_copy(h).wait_recv()

        came = jnp.where(c == 0, ret_in[h].astype(F32), 0.0)
        grad[1, h, pl.ds(band - reach, reach)] = ((pending + came) * inverse).astype(BF16)
        edge_copy(h, 1).start()

    def gathered(i, goal):
        total = None
        for b in (0, 1, -1):
            inner = None
            enter = None
            for a in (-1, 0, 1):
                h = goal - a
                if not 0 <= h < depth:
                    continue
                lanes = pl.ds(((a + 1) * 3 + b + 1) * cin, cin)
                main = zed[i, h, 0:band, lanes]
                inner = main if inner is None else inner + main
                if b != 0:
                    line = zed[i, h, pl.ds(band, TILE), lanes]
                    enter = line if enter is None else enter + line
            if b == 0:
                total = inner
            elif b == 1:
                entering = jnp.where(c == 1, enter[TILE - 1 : TILE], 0.0)
                total = total + shifted(inner, 1, entering)
            else:
                entering = jnp.where(c == 0, enter[0:1], 0.0)
                total = total + shifted(inner, -1, entering)
        return total

    for load in loads[4:]:
        load.wait()
    for i in (1, 0):
        tile_mid(i).wait_recv()
        for framed in range(1, depth + 1):
            lay(framed, i)
    for i in (1, 0):
        for h in range(depth):
            own_conv[i, h] = convolve(i, h, *own_taps(h))

    @pl.when(has_down)
    def _():
        for i in (1, 0):
            tile_down(i).wait_send()
            down(i).wait_send()

    @pl.when(has_up)
    def _():
        for i in (1, 0):
            tile_up(i).start()
            up(i).start()

    hear_word(0)
    if rounds > 1:
        spread_word(1)

    def from_above(i):
        @pl.when(has_up)
        def _():
            tile_down(i).wait_recv()
            down(i).wait_recv()

        lay(0, i)

    def from_below(i):
        @pl.when(has_down)
        def _():
            tile_up(i).wait_recv()
            up(i).wait_recv()

        lay(depth + 1, i)

    def ready_part(side, goal, i):
        part_out[side, i] = gathered(i, goal).astype(BF16)

    def give(side, allowed, i):
        @pl.when(allowed)
        def _():
            part_copy(side, i).start()

    def entering(h, i):
        if h == 0:
            from_above(i)
        if h == depth - 1:
            from_below(i)

    def pair_copy(k):
        return remote(pair_out.at[k, other], pair_in.at[k], pair_send.at[k], pair_recv.at[k], r, other)

    scale = 1.0 / math.sqrt(2 * depth * band * group)
    for h in range(depth):
        entering(h, 1)
        left_chain(h)
        if h == 0:
            spread_edge(0, 0)
            ready_part(0, -1, 0)
            give(0, has_up, 0)
        entering(h, 0)
        right_chain(h)
        if h == depth - 1:
            for k in range(3):
                lanes = pl.ds(k * 3 * cin, 3 * cin)
                total = matmul(grad[1, h], patch[1, h, :, lanes], ((0,), (0,)))
                total = (early[:, lanes] + total) * scale
                for s in range(rows):
                    for col in range(cols):
                        start = (s * cols + col) * quota
                        piece = total[start : start + quota]
                        acc[k, col, s % 2, s // 2] = piece
                        pair_out[k, col, s % 2, s // 2] = piece.astype(BF16)
                pair_copy(k).start()
        spread_grad(1, h)
        if h > 0:
            spread_edge(0, h)
        spread_edge(1, h)
        if h == 0:
            ready_part(0, -1, 1)
            give(0, has_up, 1)
            if rounds > 1:
                hear_word(1)
            if rounds > 2:
                spread_word(2)
    for k in range(2, rounds):
        hear_word(k)
        if k + 1 < rounds:
            spread_word(k + 1)

    half = rows // 2
    place_in_half = r // 2
    parity = lax.rem(r, 2)
    across = r + 1 - 2 * parity

    def cross_copy(k):
        return remote(cross_out.at[k], cross_in.at[k], cross_send.at[k], cross_recv.at[k], across, c)

    def chunk_copy(k, i):
        goal = lax.rem(place_in_half + i, half)
        return remote(
            chunk.at[k, goal], landed.at[k, i], chunk_send.at[k, i], chunk_recv.at[k, i], 2 * goal + parity, c
        )

    for k in range(3):
        pair_copy(k).wait_recv()
        cross_out[k] = (acc[k, c, 1 - parity] + pair_in[k, 1 - parity].astype(F32)).astype(BF16)
        cross_copy(k).start()
        acc[k, c, parity] += pair_in[k, parity].astype(F32)


    outs = (gl_buf, gr_buf)

    def store(i, goal):
        return pltpu.make_async_copy(outs[i].at[goal], (gl_out, gr_out)[i].at[goal], store_sem.at[i, goal])

    def put(goal):
        for i in (0, 1):
            total = own_conv[i, goal, :, 0:cin]
            if goal == 0:
                total = total + jnp.where(has_up, part_in[0, i].astype(F32), 0.0)
            if goal == depth - 1:
                total = total + jnp.where(has_down, part_in[1, i].astype(F32), 0.0)
            outs[i][goal] = total.astype(BF16)
            store(i, goal).start()

    def last_copy(k):
        return remote(whole.at[k, c], whole.at[k, c], whole_send.at[k], whole_recv.at[k], r, other)

    for i in (0, 1):
        ready_part(1, depth, i)
        for goal in range(depth):
            own_conv[i, goal, :, 0:cin] = gathered(i, goal)

    for k in range(3):
        cross_copy(k).wait_recv()
        total = acc[k, c, parity] + cross_in[k].astype(F32)
        acc[k, c, parity] = total
        chunk[k] = total.astype(BF16)

        def start_chunk(i, carry):
            chunk_copy(k, i).start()
            return carry

        lax.fori_loop(1, half, start_chunk, 0)
        if k > 0:
            give(1, has_down, k - 1)


    @pl.when(has_down)
    def _():
        for i in (0, 1):
            part_copy(0, i).wait_recv()

    for goal in range(depth - 1, 0, -1):
        put(goal)

    for k in range(3):

        def wait_chunk(i, carry):
            chunk_copy(k, i).wait_recv()
            return carry

        def add_chunk(i, total):
            return total + landed[k, i].astype(F32)

        lax.fori_loop(1, half, wait_chunk, 0)
        whole[k, c] = lax.fori_loop(1, half, add_chunk, acc[k, c, parity, place_in_half])
        last_copy(k).start()

    @pl.when(has_up)
    def _():
        for i in (0, 1):
            part_copy(1, i).wait_recv()

    put(0)

    for k in range(3):
        last_copy(k).wait_recv()
        for col in range(cols):
            wg_buf[pl.ds(col * quota, quota), pl.ds(k * 3 * cin, 3 * cin)] = whole[k, col]

    whole_store = pltpu.make_async_copy(wg_buf, wg_out, load_sem.at[0])
    whole_store.start()
    for k in range(3):
        last_copy(k).wait_send()
        pair_copy(k).wait_send()
        cross_copy(k).wait_send()

        def drain(i, carry):
            chunk_copy(k, i).wait_send()
            return carry

        lax.fori_loop(1, half, drain, 0)
    for i in (0, 1):
        tile_mid(i).wait_send()
    for h in range(depth):
        for i in (0, 1):
            edge_copy(h, i).wait_send()

    @pl.when(has_down)
    def _():
        for i in (0, 1):
            part_copy(1, i).wait_send()

    @pl.when(has_up)
    def _():
        for i in (0, 1):
            tile_up(i).wait_send()
            up(i).wait_send()
            part_copy(0, i).wait_send()

    @pl.when(c == 0)
    def _():
        for h in range(depth):
            ext_copy(h).wait_send()

    @pl.when(c == 1)
    def _():
        for h in range(depth):
            ret_copy(h).wait_send()

    for i in (0, 1):
        for goal in range(depth):
            store(i, goal).wait()
    whole_store.wait()


def hand_over(a, b, w, a_out, b_out, w_out, a_mid, b_mid, w_mid, sem_in, sem_out):
    into = [
        pltpu.make_async_copy(src, mid, sem_in.at[k])
        for k, (src, mid) in enumerate(((a, a_mid), (b, b_mid), (w, w_mid)))
    ]
    out = [
        pltpu.make_async_copy(mid, dst, sem_out.at[k])
        for k, (mid, dst) in enumerate(((a_mid, a_out), (b_mid, b_out), (w_mid, w_out)))
    ]
    for copy in into:
        copy.start()
    for first, second in zip(into, out):
        first.wait()
        second.start()
    for copy in out:
        copy.wait()


def on_device(rows, cols, left, right, weight, l0, l1, l2, l3):
    depth, band, cin = left.shape
    taps, features = weight.shape
    reach = l0.shape[2]
    blocks = band // reach
    quota = features // (rows * cols)
    third = taps // 3
    l2 = jnp.swapaxes(l2, 1, 2)
    l3 = jnp.swapaxes(l3, 1, 2)
    dma = pltpu.SemaphoreType.DMA
    results = pl.pallas_call(
        functools.partial(kernel, rows, cols),
        out_shape=(
            jax.ShapeDtypeStruct(left.shape, BF16),
            jax.ShapeDtypeStruct(right.shape, BF16),
            jax.ShapeDtypeStruct((features // rows, taps), F32),
        ),
        in_specs=[pl.BlockSpec(memory_space=pl.ANY)] * 7,
        out_specs=(pl.BlockSpec(memory_space=pl.ANY),) * 3,
        scratch_shapes=[
            *(pltpu.VMEM(x.shape, BF16) for x in (left, right, left, right)),
            pltpu.VMEM((features // rows, taps), F32),
            *(pltpu.VMEM(x.shape, BF16) for x in (weight, l0, l1, l2, l3)),
            pltpu.VMEM((2, 2, band, cin), BF16),
            pltpu.VMEM((2, depth + 2, TILE, cin), BF16),
            pltpu.VMEM((depth, blocks, reach, 2 * reach), BF16),
            pltpu.VMEM((2, depth, band, taps), BF16),
            pltpu.VMEM((band, features), BF16),
            pltpu.VMEM((depth, reach + band, features), BF16),
            pltpu.VMEM((depth, reach, features), BF16),
            pltpu.VMEM((depth, reach, features), BF16),
            pltpu.VMEM((2, depth, band, features), BF16),
            pltpu.VMEM((2, depth, TILE, features), BF16),
            pltpu.VMEM((2, depth, band + TILE, taps), F32),
            pltpu.VMEM((2, 2, band, cin), BF16),
            pltpu.VMEM((2, 2, band, cin), BF16),
            pltpu.VMEM((2, depth, band, features), F32),
            pltpu.VMEM((3, cols, 2, rows // 2, quota, third), F32),
            pltpu.VMEM((features, taps), F32),
            pltpu.VMEM((3, cols, 2, rows // 2, quota, third), BF16),
            pltpu.VMEM((3, 2, rows // 2, quota, third), BF16),
            *(pltpu.VMEM((3, rows // 2, quota, third), BF16) for _ in range(4)),
            pltpu.VMEM((3, cols, quota, third), F32),
            dma((2, 2)), dma((2, 2)), dma((3, 2)), dma((3, 2)),
            dma((depth,)), dma((depth,)), dma((depth,)), dma((depth,)),
            dma((2, depth)), dma((2, depth)), dma((2, 2)), dma((2, 2)),
            dma((3,)), dma((3,)), dma((3,)), dma((3,)), dma((3, rows // 2)), dma((3, rows // 2)), dma((3,)), dma((3,)), dma((7,)),
            dma((2, depth)), pltpu.SemaphoreType.REGULAR(((rows - 1).bit_length(), 2)),
        ],
        compiler_params=pltpu.CompilerParams(
            collective_id=0, has_side_effects=True, vmem_limit_bytes=60 * 1024 * 1024
        ),
        name="stereo_backward",
    )(left, right, weight, l0, l1, l2, l3)
    hbm = pl.BlockSpec(memory_space=pl.ANY)
    shapes = tuple(jax.ShapeDtypeStruct(x.shape, x.dtype) for x in results)
    return pl.pallas_call(
        hand_over,
        out_shape=shapes,
        in_specs=[hbm] * 3,
        out_specs=(hbm,) * 3,
        scratch_shapes=[*(pltpu.VMEM(x.shape, x.dtype) for x in results), dma((3,)), dma((3,))],
        name="hand_over",
    )(*results)


def solution(mesh):
    banded = P(("pairs", "rows"), "cols", None)
    return jax.shard_map(
        functools.partial(on_device, mesh.shape["rows"], mesh.shape["cols"]),
        mesh=mesh,
        in_specs=(banded, banded, P(), banded, banded, banded, banded),
        out_specs=(banded, banded, P(("pairs", "rows"), None)),
        check_vma=False,
    )
```

```python
import functools
import math

import jax
import jax.numpy as jnp
from jax import lax
from jax.experimental import pallas as pl
from jax.experimental.pallas import tpu as pltpu
from jax.sharding import PartitionSpec as P

F32 = jnp.float32
BF16 = jnp.bfloat16
TILE = 16


def remote(src, dst, send, recv, row, col):
    return pltpu.make_async_remote_copy(
        src_ref=src,
        dst_ref=dst,
        send_sem=send,
        recv_sem=recv,
        device_id={"rows": row, "cols": col},
        device_id_type=pl.DeviceIdType.MESH,
    )


def matmul(a, b, dims):
    return lax.dot_general(a, b, (dims, ((), ())), preferred_element_type=F32)


def expansion(levels, reach, factor):
    source = lax.broadcasted_iota(jnp.int32, (levels, reach), 0)
    target = (reach - 1) - lax.broadcasted_iota(jnp.int32, (levels, reach), 1)
    bits = factor.bit_length() - 1
    hit = lax.shift_right_logical(target, jnp.int32(bits)) == source
    return jnp.where(hit, 1.0 / factor, 0.0).astype(BF16)


def kernel(
    rows, cols, left_hbm, right_hbm, weight_hbm, l0_hbm, l1_hbm, l2_hbm, l3_hbm, gl_out, gr_out, wg_out,
    left, right, gl_buf, gr_buf, wg_buf, weight, l0, l1, l2, l3, halo_row, halo_col, band_m, patch, left_feat, right_ext, ret_out, ret_in,
    grad, grad_edge, zed, part_out, part_in, own_conv, acc, early, pair_out, pair_in, cross_out, cross_in, chunk, landed, whole,
    row_send, row_recv, col_send, col_recv, ext_send, ext_recv, ret_send, ret_recv,
    edge_send, edge_recv, part_send, part_recv, pair_send, pair_recv, cross_send, cross_recv, chunk_send, chunk_recv, whole_send, whole_recv, load_sem, store_sem, known,
):
    depth, band, cin = left.shape
    features = weight.shape[1]
    reach = l0.shape[2]
    blocks = band // reach
    quota = features // (rows * cols)
    r = lax.axis_index("rows")
    c = lax.axis_index("cols")
    other = 1 - c
    images = (left, right)
    sources = (left_hbm, right_hbm)
    group = rows * cols
    has_up = r > 0
    has_down = r < rows - 1

    barrier = pltpu.get_barrier_semaphore()

    def tell(semaphore, row, col):
        pl.semaphore_signal(
            semaphore, inc=1, device_id={"rows": row, "cols": col}, device_id_type=pl.DeviceIdType.MESH
        )

    tell(barrier, r, other)

    @pl.when(has_up)
    def _():
        for col in (c, other):
            tell(barrier, r - 1, col)

    @pl.when(has_down)
    def _():
        for col in (c, other):
            tell(barrier, r + 1, col)

    loads = [
        pltpu.make_async_copy(src, dst, load_sem.at[k])
        for k, (src, dst) in enumerate(
            (
                (l0_hbm, l0), (l1_hbm, l1), (l2_hbm, l2), (l3_hbm, l3),
                (right_hbm, right), (left_hbm, left), (weight_hbm, weight),
            )
        )
    ]
    for load in loads:
        load.start()
    pl.semaphore_wait(barrier, 1 + 2 * has_up.astype(jnp.int32) + 2 * has_down.astype(jnp.int32))

    rounds = (rows - 1).bit_length()

    def spread_word(k):
        @pl.when(r >= 2**k)
        def _():
            tell(known.at[k, 1], r - 2**k, c)

        @pl.when(r + 2**k < rows)
        def _():
            tell(known.at[k, 0], r + 2**k, c)

    def hear_word(k):
        @pl.when(r >= 2**k)
        def _():
            pl.semaphore_wait(known.at[k, 0], 1)

        @pl.when(r + 2**k < rows)
        def _():
            pl.semaphore_wait(known.at[k, 1], 1)

    near = pl.multiple_of(other * (band - TILE), TILE)

    def down(i):
        return remote(sources[i].at[depth - 1], halo_row.at[0, i], row_send.at[0, i], row_recv.at[0, i], r + 1, c)

    def up(i):
        return remote(sources[i].at[0], halo_row.at[1, i], row_send.at[1, i], row_recv.at[1, i], r - 1, c)

    def tile_mid(i):
        return remote(
            sources[i].at[:, pl.ds(near, TILE)], halo_col.at[i, pl.ds(1, depth)],
            col_send.at[0, i], col_recv.at[0, i], r, other,
        )

    def tile_down(i):
        return remote(
            sources[i].at[depth - 1, pl.ds(near, TILE)], halo_col.at[i, 0],
            col_send.at[1, i], col_recv.at[1, i], r + 1, other,
        )

    def tile_up(i):
        return remote(
            sources[i].at[0, pl.ds(near, TILE)], halo_col.at[i, depth + 1],
            col_send.at[2, i], col_recv.at[2, i], r - 1, other,
        )

    for i in (1, 0):
        tile_mid(i).start()

    @pl.when(has_down)
    def _():
        for i in (1, 0):
            tile_down(i).start()
            down(i).start()

    spread_word(0)

    @pl.when(r == 0)
    def _():
        halo_row[0] = jnp.zeros_like(halo_row[0])
        for i in (0, 1):
            halo_col[i, 0] = jnp.zeros_like(halo_col[i, 0])

    @pl.when(r == rows - 1)
    def _():
        halo_row[1] = jnp.zeros_like(halo_row[1])
        for i in (0, 1):
            halo_col[i, depth + 1] = jnp.zeros_like(halo_col[i, depth + 1])

    spread = [expansion(count, reach, reach // count) for count in (reach, l1.shape[2], l2.shape[1], l3.shape[1])]
    for load in loads[:4]:
        load.wait()
    for h in range(depth):
        for s in range(blocks):
            at = pl.ds(s * reach, reach)
            total = matmul(l0[h, at], spread[0], ((1,), (0,)))
            total = total + matmul(l1[h, at], spread[1], ((1,), (0,)))
            for level, way in zip((l2, l3), spread[2:]):
                total = total + matmul(level[h, :, at], way, ((0,), (0,)))
            total = total.astype(BF16).astype(F32)
            wide = jnp.concatenate([total, jnp.zeros_like(total)], axis=1)
            band_m[h, s] = pltpu.roll(wide, 1, 1, stride=1, stride_axis=0).astype(BF16)

    place = lax.broadcasted_iota(jnp.int32, (band, cin), 0)

    def shifted(x, by, edge):
        if by == 1:
            return jnp.where(place == 0, edge, pltpu.roll(x, 1, 0))
        return jnp.where(place == band - 1, edge, pltpu.roll(x, band - 1, 0))

    def lay(framed, i):
        if framed == 0:
            base = halo_row[0, i]
        elif framed == depth + 1:
            base = halo_row[1, i]
        else:
            base = images[i][framed - 1]
        tile = halo_col[i, framed].astype(F32)
        zero = jnp.zeros((1, cin), F32)
        enter_left = jnp.where(c == 0, zero, tile[TILE - 1 : TILE])
        enter_right = jnp.where(c == 0, tile[0:1], zero)
        wide = base.astype(F32)
        three = (
            shifted(wide, 1, enter_left).astype(BF16),
            base,
            shifted(wide, -1, enter_right).astype(BF16),
        )
        for row_tap in range(3):
            h = framed - row_tap
            if 0 <= h < depth:
                for k in range(3):
                    patch[i, h, :, pl.ds((row_tap * 3 + k) * cin, cin)] = three[k]

    inverse = 1.0 / math.sqrt(features)

    def ext_copy(h):
        return remote(
            right_ext.at[h, pl.ds(band, reach)], right_ext.at[h, pl.ds(0, reach)],
            ext_send.at[h], ext_recv.at[h], r, other,
        )

    def ret_copy(h):
        return remote(ret_out.at[h], ret_in.at[h], ret_send.at[h], ret_recv.at[h], r, other)

    def edge_copy(h, i):
        return remote(
            grad.at[i, h, pl.ds(near, TILE)], grad_edge.at[i, h], edge_send.at[i, h], edge_recv.at[i, h], r, other
        )

    def part_copy(side, i):
        target = r - 1 if side == 0 else r + 1
        return remote(
            part_out.at[side, i], part_in.at[1 - side, i], part_send.at[side, i], part_recv.at[1 - side, i],
            target, c,
        )

    @pl.when(c == 0)
    def _():
        right_ext[:, 0:reach] = jnp.zeros((depth, reach, features), BF16)

    def own_taps(h):
        return (0 if h > 0 else 1), (3 if h < depth - 1 else 2)

    def convolve(i, h, first, last):
        lanes = pl.ds(first * 3 * cin, (last - first) * 3 * cin)
        return matmul(patch[i, h, :, lanes], weight[lanes], ((1,), (0,)))

    def feature(i, h):
        first, last = own_taps(h)
        total = own_conv[i, h]
        if first > 0:
            total = total + convolve(i, h, 0, first)
        if last < 3:
            total = total + convolve(i, h, last, 3)
        return total.astype(BF16)

    def weight_term(i, h):
        return matmul(grad[i, h], patch[i, h], ((0,), (0,)))

    def spread_grad(i, h):
        zed[i, h, 0:band] = matmul(grad[i, h], weight[...], ((1,), (1,)))

    def spread_edge(i, h):
        edge_copy(h, i).wait_recv()
        zed[i, h, pl.ds(band, TILE)] = matmul(grad_edge[i, h], weight[...], ((1,), (1,)))

    def left_chain(h):
        right_ext[h, pl.ds(reach, band)] = feature(1, h)

        @pl.when(c == 0)
        def _():
            ext_copy(h).start()

        for s in range(blocks - 1, -1, -1):
            if s == 0:
                if h > 0:
                    early[...] += weight_term(1, h - 1)

                @pl.when(c == 1)
                def _():
                    ext_copy(h).wait_recv()

            window = right_ext[h, pl.ds(s * reach, 2 * reach)]
            out = matmul(band_m[h, s], window, ((1,), (0,)))
            grad[0, h, pl.ds(s * reach, reach)] = (out * inverse).astype(BF16)
        edge_copy(h, 0).start()
        spread_grad(0, h)

    def right_chain(h):
        left_feat[...] = feature(0, h)
        pending = None
        for s in range(blocks):
            both = matmul(band_m[h, s], left_feat[pl.ds(s * reach, reach)], ((0,), (0,)))
            head = both[:reach]
            if s == 0:
                ret_out[h] = head.astype(BF16)

                @pl.when(c == 1)
                def _():
                    ret_copy(h).start()
            else:
                grad[1, h, pl.ds((s - 1) * reach, reach)] = ((pending + head) * inverse).astype(BF16)
            pending = both[reach:]

        if h == 0:
            early[...] = weight_term(0, h)
        else:
            early[...] += weight_term(0, h)

        @pl.when(c == 0)
        def _():
            ret_copy(h).wait_recv()

        came = jnp.where(c == 0, ret_in[h].astype(F32), 0.0)
        grad[1, h, pl.ds(band - reach, reach)] = ((pending + came) * inverse).astype(BF16)
        edge_copy(h, 1).start()

    def gathered(i, goal):
        total = None
        for b in (0, 1, -1):
            inner = None
            enter = None
            for a in (-1, 0, 1):
                h = goal - a
                if not 0 <= h < depth:
                    continue
                lanes = pl.ds(((a + 1) * 3 + b + 1) * cin, cin)
                main = zed[i, h, 0:band, lanes]
                inner = main if inner is None else inner + main
                if b != 0:
                    line = zed[i, h, pl.ds(band, TILE), lanes]
                    enter = line if enter is None else enter + line
            if b == 0:
                total = inner
            elif b == 1:
                entering = jnp.where(c == 1, enter[TILE - 1 : TILE], 0.0)
                total = total + shifted(inner, 1, entering)
            else:
                entering = jnp.where(c == 0, enter[0:1], 0.0)
                total = total + shifted(inner, -1, entering)
        return total

    for load in loads[4:]:
        load.wait()
    for i in (1, 0):
        tile_mid(i).wait_recv()
        for framed in range(1, depth + 1):
            lay(framed, i)
    for i in (1, 0):
        for h in range(depth):
            own_conv[i, h] = convolve(i, h, *own_taps(h))

    @pl.when(has_down)
    def _():
        for i in (1, 0):
            tile_down(i).wait_send()
            down(i).wait_send()

    @pl.when(has_up)
    def _():
        for i in (1, 0):
            tile_up(i).start()
            up(i).start()

    hear_word(0)
    if rounds > 1:
        spread_word(1)

    def from_above(i):
        @pl.when(has_up)
        def _():
            tile_down(i).wait_recv()
            down(i).wait_recv()

        lay(0, i)

    def from_below(i):
        @pl.when(has_down)
        def _():
            tile_up(i).wait_recv()
            up(i).wait_recv()

        lay(depth + 1, i)

    def ready_part(side, goal, i):
        part_out[side, i] = gathered(i, goal).astype(BF16)

    def give(side, allowed, i):
        @pl.when(allowed)
        def _():
            part_copy(side, i).start()

    def entering(h, i):
        if h == 0:
            from_above(i)
        if h == depth - 1:
            from_below(i)

    def pair_copy(k):
        return remote(pair_out.at[k, other], pair_in.at[k], pair_send.at[k], pair_recv.at[k], r, other)

    scale = 1.0 / math.sqrt(2 * depth * band * group)
    for h in range(depth):
        entering(h, 1)
        left_chain(h)
        if h == 0:
            spread_edge(0, 0)
            ready_part(0, -1, 0)
            give(0, has_up, 0)
        entering(h, 0)
        right_chain(h)
        if h == depth - 1:
            for k in range(3):
                lanes = pl.ds(k * 3 * cin, 3 * cin)
                total = matmul(grad[1, h], patch[1, h, :, lanes], ((0,), (0,)))
                total = (early[:, lanes] + total) * scale
                for s in range(rows):
                    for col in range(cols):
                        start = (s * cols + col) * quota
                        piece = total[start : start + quota]
                        acc[k, col, s % 2, s // 2] = piece
                        pair_out[k, col, s % 2, s // 2] = piece.astype(BF16)
                pair_copy(k).start()
        spread_grad(1, h)
        if h > 0:
            spread_edge(0, h)
        spread_edge(1, h)
        if h == 0:
            ready_part(0, -1, 1)
            give(0, has_up, 1)
            if rounds > 1:
                hear_word(1)
            if rounds > 2:
                spread_word(2)
    for k in range(2, rounds):
        hear_word(k)
        if k + 1 < rounds:
            spread_word(k + 1)

    half = rows // 2
    place_in_half = r // 2
    parity = lax.rem(r, 2)
    across = r + 1 - 2 * parity

    def cross_copy(k):
        return remote(cross_out.at[k], cross_in.at[k], cross_send.at[k], cross_recv.at[k], across, c)

    def chunk_copy(k, i):
        goal = lax.rem(place_in_half + i, half)
        return remote(
            chunk.at[k, goal], landed.at[k, i], chunk_send.at[k, i], chunk_recv.at[k, i], 2 * goal + parity, c
        )

    for k in range(3):
        pair_copy(k).wait_recv()
        cross_out[k] = (acc[k, c, 1 - parity] + pair_in[k, 1 - parity].astype(F32)).astype(BF16)
        cross_copy(k).start()
        acc[k, c, parity] += pair_in[k, parity].astype(F32)


    outs = (gl_buf, gr_buf)

    def store(i, goal):
        return pltpu.make_async_copy(outs[i].at[goal], (gl_out, gr_out)[i].at[goal], store_sem.at[i, goal])

    def put(goal):
        for i in (0, 1):
            total = own_conv[i, goal, :, 0:cin]
            if goal == 0:
                total = total + jnp.where(has_up, part_in[0, i].astype(F32), 0.0)
            if goal == depth - 1:
                total = total + jnp.where(has_down, part_in[1, i].astype(F32), 0.0)
            outs[i][goal] = total.astype(BF16)
            store(i, goal).start()

    def last_copy(k):
        return remote(whole.at[k, c], whole.at[k, c], whole_send.at[k], whole_recv.at[k], r, other)

    for i in (0, 1):
        ready_part(1, depth, i)
        for goal in range(depth):
            own_conv[i, goal, :, 0:cin] = gathered(i, goal)

    for k in range(3):
        cross_copy(k).wait_recv()
        total = acc[k, c, parity] + cross_in[k].astype(F32)
        acc[k, c, parity] = total
        chunk[k] = total.astype(BF16)

        def start_chunk(i, carry):
            chunk_copy(k, i).start()
            return carry

        lax.fori_loop(1, half, start_chunk, 0)
        if k == 1:
            give(1, has_down, 0)


    @pl.when(has_down)
    def _():
        for i in (0, 1):
            part_copy(0, i).wait_recv()

    for goal in range(depth - 1, 0, -1):
        put(goal)

    for k in range(3):

        def wait_chunk(i, carry):
            chunk_copy(k, i).wait_recv()
            return carry

        def add_chunk(i, total):
            return total + landed[k, i].astype(F32)

        lax.fori_loop(1, half, wait_chunk, 0)
        whole[k, c] = lax.fori_loop(1, half, add_chunk, acc[k, c, parity, place_in_half])
        last_copy(k).start()
        if k == 0:
            give(1, has_down, 1)

    @pl.when(has_up)
    def _():
        for i in (0, 1):
            part_copy(1, i).wait_recv()

    put(0)

    for k in range(3):
        last_copy(k).wait_recv()
        for col in range(cols):
            wg_buf[pl.ds(col * quota, quota), pl.ds(k * 3 * cin, 3 * cin)] = whole[k, col]

    whole_store = pltpu.make_async_copy(wg_buf, wg_out, load_sem.at[0])
    whole_store.start()
    for k in range(3):
        last_copy(k).wait_send()
        pair_copy(k).wait_send()
        cross_copy(k).wait_send()

        def drain(i, carry):
            chunk_copy(k, i).wait_send()
            return carry

        lax.fori_loop(1, half, drain, 0)
    for i in (0, 1):
        tile_mid(i).wait_send()
    for h in range(depth):
        for i in (0, 1):
            edge_copy(h, i).wait_send()

    @pl.when(has_down)
    def _():
        for i in (0, 1):
            part_copy(1, i).wait_send()

    @pl.when(has_up)
    def _():
        for i in (0, 1):
            tile_up(i).wait_send()
            up(i).wait_send()
            part_copy(0, i).wait_send()

    @pl.when(c == 0)
    def _():
        for h in range(depth):
            ext_copy(h).wait_send()

    @pl.when(c == 1)
    def _():
        for h in range(depth):
            ret_copy(h).wait_send()

    for i in (0, 1):
        for goal in range(depth):
            store(i, goal).wait()
    whole_store.wait()


def hand_over(a, b, w, a_out, b_out, w_out, a_mid, b_mid, w_mid, sem_in, sem_out):
    into = [
        pltpu.make_async_copy(src, mid, sem_in.at[k])
        for k, (src, mid) in enumerate(((a, a_mid), (b, b_mid), (w, w_mid)))
    ]
    out = [
        pltpu.make_async_copy(mid, dst, sem_out.at[k])
        for k, (mid, dst) in enumerate(((a_mid, a_out), (b_mid, b_out), (w_mid, w_out)))
    ]
    for copy in into:
        copy.start()
    for first, second in zip(into, out):
        first.wait()
        second.start()
    for copy in out:
        copy.wait()


def on_device(rows, cols, left, right, weight, l0, l1, l2, l3):
    depth, band, cin = left.shape
    taps, features = weight.shape
    reach = l0.shape[2]
    blocks = band // reach
    quota = features // (rows * cols)
    third = taps // 3
    l2 = jnp.swapaxes(l2, 1, 2)
    l3 = jnp.swapaxes(l3, 1, 2)
    dma = pltpu.SemaphoreType.DMA
    results = pl.pallas_call(
        functools.partial(kernel, rows, cols),
        out_shape=(
            jax.ShapeDtypeStruct(left.shape, BF16),
            jax.ShapeDtypeStruct(right.shape, BF16),
            jax.ShapeDtypeStruct((features // rows, taps), F32),
        ),
        in_specs=[pl.BlockSpec(memory_space=pl.ANY)] * 7,
        out_specs=(pl.BlockSpec(memory_space=pl.ANY),) * 3,
        scratch_shapes=[
            *(pltpu.VMEM(x.shape, BF16) for x in (left, right, left, right)),
            pltpu.VMEM((features // rows, taps), F32),
            *(pltpu.VMEM(x.shape, BF16) for x in (weight, l0, l1, l2, l3)),
            pltpu.VMEM((2, 2, band, cin), BF16),
            pltpu.VMEM((2, depth + 2, TILE, cin), BF16),
            pltpu.VMEM((depth, blocks, reach, 2 * reach), BF16),
            pltpu.VMEM((2, depth, band, taps), BF16),
            pltpu.VMEM((band, features), BF16),
            pltpu.VMEM((depth, reach + band, features), BF16),
            pltpu.VMEM((depth, reach, features), BF16),
            pltpu.VMEM((depth, reach, features), BF16),
            pltpu.VMEM((2, depth, band, features), BF16),
            pltpu.VMEM((2, depth, TILE, features), BF16),
            pltpu.VMEM((2, depth, band + TILE, taps), F32),
            pltpu.VMEM((2, 2, band, cin), BF16),
            pltpu.VMEM((2, 2, band, cin), BF16),
            pltpu.VMEM((2, depth, band, features), F32),
            pltpu.VMEM((3, cols, 2, rows // 2, quota, third), F32),
            pltpu.VMEM((features, taps), F32),
            pltpu.VMEM((3, cols, 2, rows // 2, quota, third), BF16),
            pltpu.VMEM((3, 2, rows // 2, quota, third), BF16),
            *(pltpu.VMEM((3, rows // 2, quota, third), BF16) for _ in range(4)),
            pltpu.VMEM((3, cols, quota, third), F32),
            dma((2, 2)), dma((2, 2)), dma((3, 2)), dma((3, 2)),
            dma((depth,)), dma((depth,)), dma((depth,)), dma((depth,)),
            dma((2, depth)), dma((2, depth)), dma((2, 2)), dma((2, 2)),
            dma((3,)), dma((3,)), dma((3,)), dma((3,)), dma((3, rows // 2)), dma((3, rows // 2)), dma((3,)), dma((3,)), dma((7,)),
            dma((2, depth)), pltpu.SemaphoreType.REGULAR(((rows - 1).bit_length(), 2)),
        ],
        compiler_params=pltpu.CompilerParams(
            collective_id=0, has_side_effects=True, vmem_limit_bytes=60 * 1024 * 1024
        ),
        name="stereo_backward",
    )(left, right, weight, l0, l1, l2, l3)
    hbm = pl.BlockSpec(memory_space=pl.ANY)
    shapes = tuple(jax.ShapeDtypeStruct(x.shape, x.dtype) for x in results)
    return pl.pallas_call(
        hand_over,
        out_shape=shapes,
        in_specs=[hbm] * 3,
        out_specs=(hbm,) * 3,
        scratch_shapes=[*(pltpu.VMEM(x.shape, x.dtype) for x in results), dma((3,)), dma((3,))],
        name="hand_over",
    )(*results)


def solution(mesh):
    banded = P(("pairs", "rows"), "cols", None)
    return jax.shard_map(
        functools.partial(on_device, mesh.shape["rows"], mesh.shape["cols"]),
        mesh=mesh,
        in_specs=(banded, banded, P(), banded, banded, banded, banded),
        out_specs=(banded, banded, P(("pairs", "rows"), None)),
        check_vma=False,
    )
```
